32 devices in a mesh: tm: 8 (over y, x, core), rows: 4 (over z).
Axes of the slice: x: 2, y: 2, z: 4, core: 2. Of those that a mesh axis runs over, the one named last changes fastest.
Arguments:
- frames_in: bfloat16 [32, 32, 32, 512], P('tm', 'rows'), may hold values from -6 to 6
- weight_in: bfloat16 [2, 512, 4608], P(None, 'rows'), may hold values from -0.09375 to 0.09375
- weight_out: bfloat16 [9, 2, 512, 512], P(None, None, 'rows'), may hold values from -0.015625 to 0.015625
- log_decay: float32 [512], replicated, may hold values from 0.0003125 to 0.06
- rotation: float32 [512], replicated, may hold values from -3.140625 to 3.140625
- start_state: float32 [32, 32, 2, 512], P('rows'), may hold values from -12 to 12
- skip_gain: float32 [512], replicated, may hold values from -1 to 1
Outputs:
- frames_out: bfloat16 [32, 32, 32, 512], P('tm', 'rows')
The draws below stay inside these ranges and needn't reach their ends.
All inputs are finite; a program needn't handle non-finite values.
Results may differ from the reference program's by a relative error of at most 0.0047.
Values may be sent and summed in bfloat16 or wider, within the bound.
A program may use at most 128 MiB of HBM per device.

```python
import math
import jax
import jax.numpy as jnp
from jax import lax

D = 512
P_SIZE = 512
HH = 32
WW = 32
FRAMES = 32


def levels(stream_key, shape, pieces, smallest, largest):
    level, own = 1.0, jax.random.fold_in(stream_key, 6)
    for axis_at, blocks in pieces:
        steps = jnp.exp(jax.random.uniform(jax.random.fold_in(own, axis_at), (blocks,), jnp.float32, smallest / len(pieces), largest / len(pieces)))
        level = level * jnp.repeat(steps, shape[axis_at] // blocks).reshape([-1 if axis == axis_at else 1 for axis in range(len(shape))])
    return level


def noise(own_key, extent, scale, bound, pieces=(), dtype=jnp.bfloat16):
    gain = levels(own_key, extent, pieces, -0.22, 0.18) if pieces else 1.0
    array = jax.random.normal(own_key, extent, jnp.float32) * scale * gain
    return jnp.minimum(jnp.maximum(array, -bound), bound).astype(dtype)


def setup_inputs(seed: int = 0) -> dict:
    arg_keys = jax.random.split(jax.random.key(seed), 8)
    frames_in = noise(arg_keys[0], (FRAMES, HH, WW, D), 1.0, 6.0, ((0, 8), (1, 4)))
    weight_in = noise(arg_keys[1], (2, P_SIZE, 9 * D), (9 * D) ** -0.5, 0.09375, ((1, 4),))
    weight_out = noise(arg_keys[2], (9, 2, P_SIZE, D), (16 * 18 * P_SIZE) ** -0.5, 0.015625, ((2, 4),))
    log_decay = jnp.clip(jnp.exp(jax.random.uniform(arg_keys[3], (P_SIZE,), jnp.float32, math.log(0.0003125), math.log(0.06))), 0.0003125, 0.06)
    rotation = jnp.clip(jax.random.uniform(arg_keys[4], (P_SIZE,), jnp.float32, -3.140625, 3.140625), -3.140625, 3.140625)
    start_state = noise(arg_keys[5], (HH, WW, 2, P_SIZE), 2.0, 12.0, ((0, 4),), jnp.float32)
    skip_gain = jnp.clip(jax.random.uniform(arg_keys[6], (D,), jnp.float32, -1.0, 1.0), -1.0, 1.0)
    return {"frames_in": frames_in, "weight_in": weight_in, "weight_out": weight_out, "log_decay": log_decay, "rotation": rotation, "start_state": start_state, "skip_gain": skip_gain}


def conv_same(field, weight, channels):
    height = field.shape[0]
    columns = field.shape[1]
    padded = jnp.pad(field, ((1, 1), (1, 1), (0, 0)))
    summed = jnp.zeros((height, columns, weight.shape[0]), jnp.float32)
    for tap_index in range(9):
        row_shift = tap_index // 3
        col_shift = tap_index % 3
        window = padded[row_shift:row_shift + height, col_shift:col_shift + columns, :]
        weight_tap = weight[:, tap_index * channels:(tap_index + 1) * channels]
        summed = summed + lax.dot_general(window, weight_tap, (((2,), (1,)), ((), ())), preferred_element_type=jnp.float32)
    return summed


def reference(frames_in, weight_in, weight_out, log_decay, rotation, start_state, skip_gain):
    modulus = jnp.exp(-log_decay)
    lam_re = modulus * jnp.cos(rotation)
    lam_im = modulus * jnp.sin(rotation)
    matrix_in = weight_in.reshape(2 * P_SIZE, 9 * D)
    matrix_out = weight_out.reshape(18 * P_SIZE, D).T
    driven = lax.map(lambda single: conv_same(single, matrix_in, D), frames_in)

    def advance(carried, forcing):
        state_re, state_im = carried
        new_re = lam_re * state_re - lam_im * state_im + forcing[..., :P_SIZE]
        new_im = lam_re * state_im + lam_im * state_re + forcing[..., P_SIZE:]
        return (new_re, new_im), jnp.concatenate([new_re, new_im], -1).astype(jnp.bfloat16)

    _, held = lax.scan(advance, (start_state[:, :, 0, :], start_state[:, :, 1, :]), driven)
    mixing = lax.map(lambda single: conv_same(single, matrix_out, 2 * P_SIZE), held)
    pre_act = mixing + skip_gain * frames_in.astype(jnp.float32)
    return jax.nn.gelu(pre_act, approximate=False).astype(jnp.bfloat16)
```

```python
import functools
import jax
import jax.numpy as jnp
from jax import lax
from jax.experimental import pallas as pl
from jax.experimental.pallas import tpu as pltpu
from jax.sharding import Mesh, PartitionSpec as P

CHIPS, CORE, ROWS = "chips", "core", "rows"


def shifted(value, axis, step):
    count = lax.axis_size(axis)
    pairs = [(i, i + step) for i in range(count) if 0 <= i + step < count]
    return lax.ppermute(value, axis, pairs)


def swapped(value):
    return lax.ppermute(value, CORE, [(0, 1), (1, 0)])


def with_halo(field):
    above = shifted(field[:, -1:], ROWS, 1)
    below = shifted(field[:, :1], ROWS, -1)
    return jnp.concatenate([above, field, below], axis=1)


def chip_at(place, chips):
    far = place // (chips // 2)
    return (1 - far) * (2 * place) + far * (2 * (chips - 1 - place) + 1)


def place_of(chip, chips):
    odd = chip % 2
    return (1 - odd) * (chip // 2) + odd * (chips - 1 - chip // 2)


def meet(chips, rows, chip, row, onward, back):
    barrier = pltpu.get_barrier_semaphore()

    def greet(**where):
        pl.semaphore_signal(
            barrier, inc=1, device_id=where, device_id_type=pl.DeviceIdType.MESH
        )

    greet(chips=onward)
    greet(chips=back)

    @pl.when(row > 0)
    def _():
        greet(rows=row - 1)

    @pl.when(row < rows - 1)
    def _():
        greet(rows=row + 1)

    sides = (row + rows - 1) // rows + (2 * rows - 2 - row) // rows
    pl.semaphore_wait(barrier, 2 + sides)


def spreader(leads, chips, rows, own_ref, full_ref, z_send, z_recv, r_send, r_recv, own_sem):
    chip, row = lax.axis_index(CHIPS), lax.axis_index(ROWS)
    place = place_of(chip, chips)
    onward = chip_at((place + 1) % chips, chips)
    back = chip_at((place + chips - 1) % chips, chips)
    many = chips // 2
    lead = (slice(None),) * leads

    def own_slice():
        return own_ref.at[lead + (chip // many, chip % many)]

    def block(shard, source, piece=None):
        at = lead + (source // many, shard, source % many)
        return full_ref.at[at if piece is None else at + (piece,)]

    keep = pltpu.make_async_copy(
        own_ref, full_ref.at[lead + (slice(None), row)], own_sem
    )

    def line(side, step):
        step_way = 1 - 2 * side
        shard = row - step_way * step
        src = own_slice() if step == 0 else block(shard, chip)
        return pltpu.make_async_remote_copy(
            src_ref=src,
            dst_ref=block(shard, chip),
            send_sem=z_send.at[side, step],
            recv_sem=z_recv.at[side, step],
            device_id={ROWS: row + step_way},
            device_id_type=pl.DeviceIdType.MESH,
        )

    def landed(side, step):
        shard = row - (1 - 2 * side) * (step + 1)
        here = block(shard, chip)
        return pltpu.make_async_remote_copy(
            src_ref=here,
            dst_ref=here,
            send_sem=z_send.at[side, step],
            recv_sem=z_recv.at[side, step],
            device_id={ROWS: row},
            device_id_type=pl.DeviceIdType.MESH,
        )

    def ring(side, step, way, turn):
        turn_way = 1 - 2 * way
        shard = row - (1 - 2 * side) * (step + 1)
        source = chip_at((place - turn_way * turn + chips) % chips, chips)
        here = block(shard, source, way)
        return pltpu.make_async_remote_copy(
            src_ref=here,
            dst_ref=here,
            send_sem=r_send.at[side, step, way, turn],
            recv_sem=r_recv.at[side, step, way, turn],
            device_id={CHIPS: back if way else onward},
            device_id_type=pl.DeviceIdType.MESH,
        )

    def ring_landed(side, step, way, turn):
        turn_way = 1 - 2 * way
        shard = row - (1 - 2 * side) * (step + 1)
        source = chip_at((place - turn_way * (turn + 1) + 2 * chips) % chips, chips)
        here = block(shard, source, way)
        return pltpu.make_async_remote_copy(
            src_ref=here,
            dst_ref=here,
            send_sem=r_send.at[side, step, way, turn],
            recv_sem=r_recv.at[side, step, way, turn],
            device_id={CHIPS: back if way else onward},
            device_id_type=pl.DeviceIdType.MESH,
        )

    def sends(side, step):
        near = row - step if side == 0 else rows - 1 - row - step
        room = rows - 1 - row if side == 0 else row
        return jnp.logical_and(near >= 0, room > 0)

    def comes(side, step):
        return (row if side == 0 else rows - 1 - row) > step

    def begin():
        keep.start()
        for side in range(2):

            @pl.when(sends(side, 0))
            def _():
                line(side, 0).start()

    def advance(tick):
        if tick < rows - 1:
            for side in range(2):

                @pl.when(comes(side, tick))
                def _():
                    landed(side, tick).wait_recv()
                    if tick + 1 < rows - 1:

                        @pl.when(sends(side, tick + 1))
                        def _():
                            line(side, tick + 1).start()

                    for way in range(2):
                        ring(side, tick, way, 0).start()

        for turn in range(1, chips):
            step = tick - turn
            if 0 <= step < rows - 1:
                for side in range(2):

                    @pl.when(comes(side, step))
                    def _():
                        for way in range(2):
                            ring_landed(side, step, way, turn - 1).wait_recv()
                            if turn < chips - 1:
                                ring(side, step, way, turn).start()

    def finish():
        for side in range(2):
            for step in range(rows - 1):

                @pl.when(sends(side, step))
                def _():
                    line(side, step).wait_send()

                @pl.when(comes(side, step))
                def _():
                    for way in range(2):
                        for turn in range(chips - 1):
                            ring(side, step, way, turn).wait_send()

    return begin, advance, finish, keep


def spread_kernel(leads, chips, rows, *refs):
    chip, row = lax.axis_index(CHIPS), lax.axis_index(ROWS)
    place = place_of(chip, chips)
    onward = chip_at((place + 1) % chips, chips)
    back = chip_at((place + chips - 1) % chips, chips)
    meet(chips, rows, chip, row, onward, back)
    begin, advance, finish, keep = spreader(leads, chips, rows, *refs)
    begin()
    for tick in range(rows - 1 + chips - 1):
        advance(tick)
    finish()
    keep.wait()


def semaphores(chips, rows):
    return [
        pltpu.SemaphoreType.DMA((2, rows - 1)),
        pltpu.SemaphoreType.DMA((2, rows - 1)),
        pltpu.SemaphoreType.DMA((2, rows - 1, 2, chips - 1)),
        pltpu.SemaphoreType.DMA((2, rows - 1, 2, chips - 1)),
        pltpu.SemaphoreType.DMA,
    ]


GROUPS = 4


def drive_kernel(chips, rows, in_ref, out_ref, field_ref, driven_ref, full_out, full_in, views, *sems):
    chip, row = lax.axis_index(CHIPS), lax.axis_index(ROWS)
    place = place_of(chip, chips)
    onward = chip_at((place + 1) % chips, chips)
    back = chip_at((place + chips - 1) % chips, chips)
    meet(chips, rows, chip, row, onward, back)
    count = len(sems) // 2
    first = spreader(0, chips, rows, in_ref, full_in, *sems[:count])
    second = spreader(1, chips, rows, out_ref, full_out, *sems[count:])
    ticks, delay = rows - 1 + chips - 1, rows - 1
    total, padded, columns, channels = field_ref.shape
    band = padded - 2
    group = total // GROUPS

    def compute(index):
        at = index * group
        taps = [
            views[b, at : at + group, a : a + band].reshape(group * band * columns, channels)
            for a in range(3)
            for b in range(3)
        ]
        window = jnp.concatenate(taps, axis=1)
        for part in range(2):
            weight = full_in[part]
            weight = weight.reshape(-1, weight.shape[-1])
            states = weight.shape[0]
            driven_ref[pl.ds(index * window.shape[0], window.shape[0]), part * states : (part + 1) * states] = (
                lax.dot_general(
                    window, weight, (((1,), (1,)), ((), ())), preferred_element_type=jnp.float32
                )
            )

    first[0]()

    @pl.loop(0, total)
    def _(frame):
        whole = field_ref[frame]
        wide = whole.astype(jnp.float32)
        edge = jnp.zeros((padded, 1, channels), jnp.float32)
        before = jnp.concatenate([edge, wide[:, : columns - 1]], axis=1)
        after = jnp.concatenate([wide[:, 1:], edge], axis=1)
        views[0, frame] = before.astype(whole.dtype)
        views[1, frame] = whole
        views[2, frame] = after.astype(whole.dtype)

    for tick in range(ticks):
        first[1](tick)
        if tick == delay - 1:
            second[0]()
        if tick >= delay:
            second[1](tick - delay)
    first[3].wait()
    for index in range(GROUPS):
        compute(index)
        if ticks - delay + index < ticks:
            second[1](ticks - delay + index)
    for tick in range(ticks - delay + GROUPS, ticks):
        second[1](tick)
    first[2]()
    second[2]()
    second[3].wait()


def drive(own_in, own_out, field, chips, rows):
    many_in = own_in.shape[:1] + (rows,) + own_in.shape[1:]
    many_out = own_out.shape[:2] + (rows,) + own_out.shape[2:]
    total, padded, columns, channels = field.shape
    pixels = total * (padded - 2) * columns
    states = many_in[1] * many_in[2] * many_in[3] * many_in[4]
    vmem = pl.BlockSpec(memory_space=pltpu.VMEM)
    return pl.pallas_call(
        functools.partial(drive_kernel, chips, rows),
        out_shape=(
            jax.ShapeDtypeStruct((pixels, 2 * states), jnp.float32),
            jax.ShapeDtypeStruct(many_out, own_out.dtype),
        ),
        in_specs=[vmem, vmem, vmem],
        out_specs=(vmem, pl.BlockSpec(memory_space=pl.ANY)),
        scratch_shapes=[
            pltpu.VMEM(many_in, own_in.dtype),
            pltpu.VMEM((3,) + field.shape, field.dtype),
        ]
        + semaphores(chips, rows)
        + semaphores(chips, rows),
        compiler_params=pltpu.CompilerParams(
            collective_id=2, has_side_effects=True, vmem_limit_bytes=60 * 1024 * 1024
        ),
    )(own_in, own_out, field)


def spread(own, leads, chips, rows, number):
    shape = own.shape[: leads + 1] + (rows,) + own.shape[leads + 1 :]
    any_space = pl.BlockSpec(memory_space=pl.ANY)
    return pl.pallas_call(
        functools.partial(spread_kernel, leads, chips, rows),
        out_shape=jax.ShapeDtypeStruct(shape, own.dtype),
        in_specs=[pl.BlockSpec(memory_space=pltpu.VMEM)],
        out_specs=any_space,
        scratch_shapes=semaphores(chips, rows),
        compiler_params=pltpu.CompilerParams(collective_id=number, has_side_effects=True),
    )(own)


def conv(field, weight, form):
    return lax.conv_general_dilated(
        field, weight, (1, 1), ((0, 0), (1, 1)),
        dimension_numbers=("NHWC", form, "NHWC"),
        preferred_element_type=jnp.float32,
    )


def recur_kernel(last_only, both_ref, begin_ref, factor_ref, result_ref):
    states = factor_ref.shape[1]
    lam_re, lam_im = factor_ref[0:1, :], factor_ref[1:2, :]
    state_re, state_im = begin_ref[0, :, :states], begin_ref[0, :, states:]
    total = both_ref.shape[0]
    for t in range(total):
        state_re, state_im = (
            lam_re * state_re - lam_im * state_im + both_ref[t, 0, :, :states],
            lam_re * state_im + lam_im * state_re + both_ref[t, 0, :, states:],
        )
        if not last_only:
            result_ref[t, 0, :, :states] = state_re.astype(result_ref.dtype)
            result_ref[t, 0, :, states:] = state_im.astype(result_ref.dtype)
    if last_only:
        result_ref[0, :, :states] = state_re.astype(result_ref.dtype)
        result_ref[0, :, states:] = state_im.astype(result_ref.dtype)


def recur(both, begin, factor, last_only):
    total, band, columns, lanes = both.shape
    frames = pl.BlockSpec((total, 1, columns, lanes), lambda i: (0, i, 0, 0))
    single = pl.BlockSpec((1, columns, lanes), lambda i: (i, 0, 0))
    shape = both.shape[1:] if last_only else both.shape
    return pl.pallas_call(
        functools.partial(recur_kernel, last_only),
        out_shape=jax.ShapeDtypeStruct(shape, jnp.bfloat16),
        grid=(band,),
        in_specs=[frames, single, pl.BlockSpec(factor.shape, lambda i: (0, 0))],
        out_specs=single if last_only else frames,
    )(both, begin, factor)


def powers(log_rate, angle, exponent):
    modulus = jnp.exp(-log_rate * exponent)
    return modulus * jnp.cos(angle * exponent), modulus * jnp.sin(angle * exponent)


ORDER = (1, 0, 2)


def power(re, im, exponent):
    out_re, out_im = jnp.ones_like(re), jnp.zeros_like(im)
    while exponent:
        if exponent % 2:
            out_re, out_im = out_re * re - out_im * im, out_re * im + out_im * re
        re, im = re * re - im * im, 2.0 * (re * im)
        exponent //= 2
    return out_re, out_im


def layer_kernel(
    win, wout, frames, begin, rate, angle, skip, out,
    views, full_in, full_out, driven, held, acc, tail, tail_half, met, joint, far_joint, given, got,
    z_send, z_recv, x_send, x_recv, y_send, y_recv,
    halo_send, halo_recv, pass_send, pass_recv, edge_send, edge_recv,
    first_send, first_recv, second_send, second_recv, swap_send, swap_recv, part_send, part_recv, local,
):
    chip, core, row = (lax.axis_index(a) for a in (CHIPS, CORE, ROWS))
    rows = lax.axis_size(ROWS)
    other = 1 - core
    beside = chip + 1 - 2 * (chip % 2)
    across = (chip + 2) % 4
    opposite = 3 - chip
    _, many, padded, columns, channels = views.shape
    band, mine = padded - 2, many // 2
    lanes = tail.shape[-1] // 2
    depth = 3 * channels
    own = row // 2 == core
    near = jnp.where(row <= 2 * core, 0, 1)
    slots = (near, 1 - near)
    here = pl.multiple_of(core * mine, mine)
    there = pl.multiple_of(other * mine, mine)
    has_up, has_down = row > 0, row < rows - 1

    def remote(src, dst, send, recv, **where):
        return pltpu.make_async_remote_copy(
            src_ref=src, dst_ref=dst, send_sem=send, recv_sem=recv,
            device_id=where, device_id_type=pl.DeviceIdType.MESH,
        )

    def block(w, slot, quarter, o):
        a = ORDER[o]
        if w == 0:
            return full_in.at[slot, :, quarter, :, a * depth : (a + 1) * depth]
        return full_out.at[a, :, slot, :, quarter]

    def source(w, quarter, o):
        a = ORDER[o]
        if w == 0:
            return win.at[:, quarter, :, a * depth : (a + 1) * depth]
        return wout.at[a, :, :, quarter]

    def z_piece(k):
        return (chip, k) if k < 3 else (opposite, 2)

    def z_copy(w, slot, k, kind, first, to):
        quarter, o = z_piece(k)
        dst = block(w, slot, quarter, o)
        src = source(w, quarter, o) if first else dst
        return remote(src, dst, z_send.at[w, kind, k], z_recv.at[w, slot, k], **{ROWS: to})

    def x_copy(w, rank, i):
        quarter, o = (chip, i) if i < 3 else (across, 1)
        ref = block(w, slots[rank], quarter, o)
        return remote(ref, ref, x_send.at[w, rank, i], x_recv.at[w, rank, i], **{CHIPS: beside})

    def y_copy(w, rank, i):
        quarter, o = (chip, i) if i < 3 else (beside, 0)
        ref = block(w, slots[rank], quarter, o)
        return remote(ref, ref, y_send.at[w, rank, i], y_recv.at[w, rank, i], **{CHIPS: across})

    def x_came(w, rank, i):
        quarter, o = (beside, i) if i < 3 else (opposite, 1)
        ref = block(w, slots[rank], quarter, o)
        remote(ref, ref, x_send.at[w, rank, i], x_recv.at[w, rank, i], **{CHIPS: beside}).wait_recv()

    def y_came(w, rank, i):
        quarter, o = (across, i) if i < 3 else (opposite, 0)
        ref = block(w, slots[rank], quarter, o)
        remote(ref, ref, y_send.at[w, rank, i], y_recv.at[w, rank, i], **{CHIPS: across}).wait_recv()

    def apart(rank):
        return jnp.logical_not(own) if rank == 0 else jnp.logical_or(own, True)

    def from_below(rank):
        return 2 * core + slots[rank] > row

    def relays(rank):
        below = from_below(rank)
        return (
            jnp.logical_and(apart(rank), jnp.logical_and(below, has_up)),
            jnp.logical_and(apart(rank), jnp.logical_and(jnp.logical_not(below), has_down)),
        )

    def guarded(rank, do):
        if rank == 0:
            pl.when(apart(0))(do)
        else:
            do()

    def send_own(w):
        for k in range(4):
            @pl.when(jnp.logical_and(own, has_up))
            def _():
                z_copy(w, near, k, 0, True, row - 1).start()

            @pl.when(jnp.logical_and(own, has_down))
            def _():
                z_copy(w, near, k, 2, True, row + 1).start()

    def z_event(w, rank, k):
        slot = slots[rank]

        def do():
            z_copy(w, slot, k, rank, False, row).wait_recv()
            if k < 3:
                x_copy(w, rank, k).start()
                y_copy(w, rank, k).start()

        guarded(rank, do)
        up, down = relays(rank)

        @pl.when(up)
        def _():
            z_copy(w, slot, k, rank, False, row - 1).start()

        @pl.when(down)
        def _():
            z_copy(w, slot, k, rank, False, row + 1).start()

    def x_event(w, rank):
        def do():
            x_came(w, rank, 0)
            y_copy(w, rank, 3).start()

        guarded(rank, do)

    def y_event(w, rank):
        def do():
            y_came(w, rank, 1)
            x_copy(w, rank, 3).start()

        guarded(rank, do)

    def events(w, rank):
        return [
            functools.partial(z_event, w, rank, 0),
            functools.partial(z_event, w, rank, 1),
            functools.partial(x_event, w, rank),
            functools.partial(z_event, w, rank, 2),
            functools.partial(y_event, w, rank),
            functools.partial(z_event, w, rank, 3),
        ]

    def complete(w, rank, o):
        def do():
            if o != 0:
                x_came(w, rank, o)
            else:
                y_came(w, rank, 3)
            if o != 1:
                y_came(w, rank, o)
            else:
                x_came(w, rank, 3)

        guarded(rank, do)

    def settle(w):
        for k in range(4):
            @pl.when(jnp.logical_and(own, has_up))
            def _():
                z_copy(w, near, k, 0, True, row - 1).wait_send()

            @pl.when(jnp.logical_and(own, has_down))
            def _():
                z_copy(w, near, k, 2, True, row + 1).wait_send()

            for rank in range(2):
                up, down = relays(rank)

                @pl.when(jnp.logical_or(up, down))
                def _():
                    z_copy(w, slots[rank], k, rank, False, row).wait_send()

        for rank in range(2):
            def do():
                for i in range(4):
                    x_copy(w, rank, i).wait_send()
                    y_copy(w, rank, i).wait_send()

            guarded(rank, do)

    barrier = pltpu.get_barrier_semaphore()

    def greet(**where):
        pl.semaphore_signal(barrier, inc=1, device_id=where, device_id_type=pl.DeviceIdType.MESH)

    greet(**{CORE: other})
    greet(**{CHIPS: beside})
    greet(**{CHIPS: across})

    @pl.when(has_up)
    def _():
        greet(**{ROWS: row - 1})

    @pl.when(has_down)
    def _():
        greet(**{ROWS: row + 1})

    pl.semaphore_wait(barrier, 3 + (row + rows - 1) // rows + (2 * rows - 2 - row) // rows)

    mine_in = views.at[1, pl.ds(here, mine), 1 : band + 1]
    keep = pltpu.make_async_copy(frames, mine_in, local.at[0])
    hold_in = pltpu.make_async_copy(win, full_in.at[near], local.at[1])
    hold_out = pltpu.make_async_copy(wout, full_out.at[:, :, near], local.at[2])
    swap = remote(frames, mine_in, swap_send, swap_recv, **{CORE: other})
    theirs_in = views.at[1, pl.ds(there, mine), 1 : band + 1]

    def halo(side, start):
        at = views.at[1, pl.ds(here, mine), band + 1 if side == 0 else 0]
        src = frames.at[:, 0 if side == 0 else band - 1]
        return remote(src, at, halo_send.at[side], halo_recv.at[side], **{ROWS: row - 1 if side == 0 else row + 1})

    def halo_at(side, first):
        return views.at[1, pl.ds(first, mine), band + 1 if side == 0 else 0]

    def halo_came(side):
        ref = halo_at(side, here)
        remote(ref, ref, halo_send.at[side], halo_recv.at[side], **{ROWS: row}).wait_recv()

    def handed(side, first):
        ref = halo_at(side, first)
        return remote(ref, ref, pass_send.at[side], pass_recv.at[side], **{CORE: other})

    gives = (has_up, has_down)
    takes = (has_down, has_up)

    swap.start()
    keep.start()
    for side in range(2):
        @pl.when(gives[side])
        def _():
            halo(side, True).start()

    send_own(0)

    @pl.when(own)
    def _():
        hold_in.start()
        hold_out.start()

    blank = jnp.zeros((columns, channels), views.dtype)
    for side in range(2):
        edge = band + 1 if side == 0 else 0

        @pl.when(jnp.logical_not(takes[side]))
        def _():
            @pl.loop(0, many)
            def _(f):
                views[1, f, edge] = blank
                for slot in range(2):
                    held[slot, 1, f, edge] = blank[:, : 2 * lanes]

    place = lax.broadcasted_iota(jnp.int32, (columns, 1), 0)
    not_first, not_last = place > 0, place < columns - 1

    def sides(wide):
        before = jnp.where(not_first, pltpu.roll(wide, 1, 0), 0.0)
        after = jnp.where(not_last, pltpu.roll(wide, columns - 1, 0), 0.0)
        return before.astype(views.dtype), after.astype(views.dtype)

    def spread_views(first, count):
        @pl.loop(0, count)
        def _(i):
            f = first + i

            @pl.loop(0, padded)
            def _(r):
                views[0, f, r], views[2, f, r] = sides(views[1, f, r].astype(jnp.float32))

    def drive(rank, o, m0, m1):
        slot, a = slots[rank], ORDER[o]

        @pl.loop(m0, m1)
        def _(m):
            at = pl.ds(m * 2, 2)
            pixels = 2 * band * columns
            window = jnp.concatenate(
                [views[b, at, a : a + band].reshape(pixels, channels) for b in range(3)], axis=1
            )
            weight = full_in[slot, :, :, :, a * depth : (a + 1) * depth].reshape(2 * lanes, depth)
            result = lax.dot_general(
                window, weight, (((1,), (1,)), ((), ())), preferred_element_type=jnp.float32
            ).reshape(2, band, columns, 2 * lanes)
            if o == 0:
                driven[slot, at] = result
            else:
                driven[slot, at] += result

    blocks = many // 2

    def factors(rank):
        at = pl.ds(2 * core + slots[rank], 1)
        modulus = jnp.exp(-rate[at, :])
        return modulus * jnp.cos(angle[at, :]), modulus * jnp.sin(angle[at, :])

    def ends(rank):
        slot = slots[rank]
        lam_re, lam_im = factors(rank)

        @pl.loop(0, band)
        def _(r):
            re, im = begin[slot, r, :, :lanes], begin[slot, r, :, lanes:]
            for t in range(many):
                re, im = (
                    lam_re * re - lam_im * im + driven[slot, t, r, :, :lanes],
                    lam_re * im + lam_im * re + driven[slot, t, r, :, lanes:],
                )
            tail[slot, r, :, :lanes] = re
            tail[slot, r, :, lanes:] = im
            tail_half[slot, r, :, :lanes] = re.astype(tail_half.dtype)
            tail_half[slot, r, :, lanes:] = im.astype(tail_half.dtype)

    tells, hears = chip < 3, chip != 2
    joins = chip < 2

    def first_copy(rank):
        slot = slots[rank]
        return remote(
            tail_half.at[slot], met.at[slot], first_send.at[rank], first_recv.at[rank], **{CHIPS: beside}
        )

    def second_copy(rank):
        slot = slots[rank]
        return remote(
            joint.at[slot], far_joint.at[slot], second_send.at[rank], second_recv.at[rank], **{CHIPS: across}
        )

    def tell(rank):
        @pl.when(tells)
        def _():
            first_copy(rank).start()

    def merge(rank):
        slot = slots[rank]
        lam_re, lam_im = factors(rank)
        jump_re, jump_im = power(lam_re, lam_im, many)

        def combine(r, late_re, late_im, early_re, early_im):
            return (
                late_re + jump_re * early_re - jump_im * early_im,
                late_im + jump_re * early_im + jump_im * early_re,
            )

        def split(ref, r):
            return ref[slot, r, :, :lanes].astype(jnp.float32), ref[slot, r, :, lanes:].astype(jnp.float32)

        def put(ref, r, value):
            ref[slot, r, :, :lanes] = value[0].astype(ref.dtype)
            ref[slot, r, :, lanes:] = value[1].astype(ref.dtype)

        @pl.when(hears)
        def _():
            first_copy(rank).wait_recv()

        @pl.when(chip == 0)
        def _():
            @pl.loop(0, band)
            def _(r):
                put(joint, r, combine(r, *split(met, r), *split(tail, r)))
                put(tail, r, split(begin, r))

        @pl.when(chip == 1)
        def _():
            @pl.loop(0, band)
            def _(r):
                put(joint, r, combine(r, *split(tail, r), *split(met, r)))
                put(tail, r, split(met, r))

        @pl.when(joins)
        def _():
            second_copy(rank).start()

    def carry(rank):
        slot = slots[rank]
        lam_re, lam_im = factors(rank)
        jump_re, jump_im = power(lam_re, lam_im, many)

        @pl.when(jnp.logical_not(joins))
        def _():
            second_copy(rank).wait_recv()

        @pl.when(chip == 2)
        def _():
            @pl.loop(0, band)
            def _(r):
                tail[slot, r] = far_joint[slot, r].astype(jnp.float32)

        @pl.when(chip == 3)
        def _():
            @pl.loop(0, band)
            def _(r):
                late, early = met[slot, r].astype(jnp.float32), far_joint[slot, r].astype(jnp.float32)
                re, im = early[:, :lanes], early[:, lanes:]
                tail[slot, r, :, :lanes] = late[:, :lanes] + jump_re * re - jump_im * im
                tail[slot, r, :, lanes:] = late[:, lanes:] + jump_re * im + jump_im * re

    def scan_rows(rank, start, count, stride):
        slot = slots[rank]
        lam_re, lam_im = factors(rank)

        @pl.loop(0, count)
        def _(i):
            r = start + i * stride
            re, im = tail[slot, r, :, :lanes], tail[slot, r, :, lanes:]
            for t in range(many):
                re, im = (
                    lam_re * re - lam_im * im + driven[slot, t, r, :, :lanes],
                    lam_re * im + lam_im * re + driven[slot, t, r, :, lanes:],
                )
                for part, value in enumerate((re, im)):
                    at = slice(part * lanes, (part + 1) * lanes)
                    before, after = sides(value)
                    held[slot, 0, t, 1 + r, :, at] = before
                    held[slot, 1, t, 1 + r, :, at] = value.astype(held.dtype)
                    held[slot, 2, t, 1 + r, :, at] = after

    def edge_copy(rank, side):
        slot = slots[rank]
        return remote(
            held.at[slot, 1, :, 1 if side == 0 else band],
            held.at[slot, 1, :, band + 1 if side == 0 else 0],
            edge_send.at[rank, side],
            edge_recv.at[slot, side],
            **{ROWS: row - 1 if side == 0 else row + 1},
        )

    def scan(rank):
        scan_rows(rank, 0, 2, band - 1)
        scan_rows(rank, 1, (band - 2) // 2, 1)
        for side in range(2):
            @pl.when(gives[side])
            def _():
                edge_copy(rank, side).start()
        scan_rows(rank, 1 + (band - 2) // 2, band - 2 - (band - 2) // 2, 1)

    def edges_came(rank):
        slot = slots[rank]
        for side in range(2):
            at = band + 1 if side == 0 else 0
            ref = held.at[slot, 1, :, at]

            @pl.when(takes[side])
            def _():
                remote(
                    ref, ref, edge_send.at[rank, side], edge_recv.at[slot, side], **{ROWS: row}
                ).wait_recv()

            @pl.loop(0, many)
            def _(f):
                held[slot, 0, f, at], held[slot, 2, f, at] = sides(held[slot, 1, f, at].astype(jnp.float32))

    def mix_block(rank, rights, first, fresh):
        slot = slots[rank]
        pixels = 2 * band * columns
        window = jnp.concatenate(
            [
                held[slot, b, pl.ds(first, 2), a : a + band].reshape(pixels, 2 * lanes)
                for a in rights
                for b in range(3)
            ],
            axis=1,
        )
        weight = jnp.concatenate([full_out[a, :, slot].reshape(6 * lanes, channels) for a in rights], axis=0)
        result = jnp.dot(window, weight, preferred_element_type=jnp.float32)
        result = result.reshape(2, band, columns, channels)
        if fresh:
            return result
        return acc[pl.ds(first, 2)] + result

    def mix(rank, rights, fresh):
        @pl.loop(0, blocks)
        def _(m):
            acc[pl.ds(m * 2, 2)] = mix_block(rank, rights, m * 2, fresh)

    def part_copy(m):
        at = pl.ds(m * 2, 2)
        return remote(
            given.at[at], got.at[at], part_send.at[m], part_recv.at[m], **{CORE: other}
        )

    def mix_last(rank, rights):
        for m in range(blocks // 2):
            given[m * 2 : m * 2 + 2] = mix_block(rank, rights, there + m * 2, False).astype(given.dtype)
            part_copy(m).start()
        for m in range(blocks // 2):
            acc[pl.ds(here + m * 2, 2)] = mix_block(rank, rights, here + m * 2, False)
        for m in range(blocks // 2):
            part_copy(m).wait_recv()

            @pl.loop(0, 2)
            def _(i):
                f = m * 2 + i

                @pl.loop(0, band)
                def _(r):
                    value = acc[here + f, r] + got[f, r].astype(jnp.float32)
                    value = value + skip[...] * views[1, here + f, 1 + r].astype(jnp.float32)
                    out[f, r] = (0.5 * value * (1.0 + lax.erf(value * 0.7071067811865476))).astype(out.dtype)

    steps = iter(events(0, 0))
    next(steps)()
    keep.wait()
    for side in range(2):
        @pl.when(takes[side])
        def _():
            halo_came(side)
            handed(side, here).start()

    next(steps)()
    spread_views(here, mine // 2)
    next(steps)()
    spread_views(here + mine // 2, mine // 2)
    next(steps)()
    remote(theirs_in, theirs_in, swap_send, swap_recv, **{CORE: other}).wait_recv()
    for side in range(2):
        @pl.when(takes[side])
        def _():
            handed(side, there).wait_recv()

    spread_views(there, mine // 2)
    next(steps)()
    spread_views(there + mine // 2, mine // 2)
    next(steps)()

    @pl.when(own)
    def _():
        hold_in.wait()
        hold_out.wait()

    steps = iter(events(0, 1))
    for o in range(3):
        next(steps)()
        complete(0, 0, o)
        drive(0, o, 0, blocks // 2)
        next(steps)()
        drive(0, o, blocks // 2, blocks)
    send_own(1)
    ends(0)
    tell(0)
    steps = iter(events(1, 0))
    complete(0, 1, 0)
    drive(1, 0, 0, blocks)
    next(steps)()
    complete(0, 1, 1)
    merge(0)
    drive(1, 1, 0, blocks)
    next(steps)()
    complete(0, 1, 2)
    drive(1, 2, 0, blocks)
    ends(1)
    tell(1)
    for step in steps:
        step()
    carry(0)
    scan(0)
    merge(1)
    steps = iter(events(1, 1))
    next(steps)()
    next(steps)()
    complete(1, 0, 0)
    mix(0, (1,), True)
    carry(1)
    scan(1)
    for step in steps:
        step()
    edges_came(0)
    complete(1, 0, 1)
    complete(1, 0, 2)
    mix(0, (0, 2), False)
    complete(1, 1, 0)
    mix(1, (1,), False)
    edges_came(1)
    complete(1, 1, 1)
    complete(1, 1, 2)
    mix_last(1, (0, 2))

    settle(0)
    settle(1)
    swap.wait_send()
    for side in range(2):
        @pl.when(gives[side])
        def _():
            halo(side, False).wait_send()
            for rank in range(2):
                edge_copy(rank, side).wait_send()

        @pl.when(takes[side])
        def _():
            handed(side, here).wait_send()

    for rank in range(2):
        @pl.when(tells)
        def _():
            first_copy(rank).wait_send()

        @pl.when(joins)
        def _():
            second_copy(rank).wait_send()

    for m in range(blocks // 2):
        part_copy(m).wait_send()


def layer(weight_in, weight_out, frames_in, start, log_decay, rotation, skip_gain):
    count, band, columns, channels = frames_in.shape
    lanes = weight_in.shape[1]
    quarter = lanes // 4
    many = 2 * count
    vmem, anywhere = pl.BlockSpec(memory_space=pltpu.VMEM), pl.BlockSpec(memory_space=pl.ANY)
    dma = pltpu.SemaphoreType.DMA
    half = frames_in.dtype
    full = jnp.float32
    return pl.pallas_call(
        layer_kernel,
        out_shape=jax.ShapeDtypeStruct(frames_in.shape, half),
        in_specs=[anywhere, anywhere, anywhere, vmem, vmem, vmem, vmem],
        out_specs=vmem,
        scratch_shapes=[
            pltpu.VMEM((3, many, band + 2, columns, channels), half),
            pltpu.VMEM((2, 2, 4, quarter, 9 * channels), half),
            pltpu.VMEM((3, 3, 2, 2, 4, quarter, channels), half),
            pltpu.VMEM((2, many, band, columns, 2 * lanes), full),
            pltpu.VMEM((2, 3, many, band + 2, columns, 2 * lanes), half),
            pltpu.VMEM((many, band, columns, channels), full),
            pltpu.VMEM((2, band, columns, 2 * lanes), full),
            pltpu.VMEM((2, band, columns, 2 * lanes), half),
            pltpu.VMEM((2, band, columns, 2 * lanes), half),
            pltpu.VMEM((2, band, columns, 2 * lanes), half),
            pltpu.VMEM((2, band, columns, 2 * lanes), half),
            pltpu.VMEM((count, band, columns, channels), half),
            pltpu.VMEM((count, band, columns, channels), half),
            dma((2, 3, 4)), dma((2, 2, 4)), dma((2, 2, 4)), dma((2, 2, 4)), dma((2, 2, 4)), dma((2, 2, 4)),
            dma((2,)), dma((2,)), dma((2,)), dma((2,)), dma((2, 2)), dma((2, 2)),
            dma((2,)), dma((2,)), dma((2,)), dma((2,)), dma, dma,
            dma((many // 4,)), dma((many // 4,)), dma((3,)),
        ],
        compiler_params=pltpu.CompilerParams(
            collective_id=3, has_side_effects=True, vmem_limit_bytes=63 * 1024 * 1024
        ),
    )(
        weight_in.reshape(2, 4, quarter, 9 * channels),
        weight_out.reshape(3, 3, 2, 4, quarter, channels),
        frames_in,
        start,
        log_decay.reshape(-1, lanes),
        rotation.reshape(-1, lanes),
        skip_gain.reshape(1, channels),
    )


def fused(frames_in, weight_in, weight_out, log_decay, rotation, start_state, skip_gain):
    core, chip = lax.axis_index(CORE), lax.axis_index(CHIPS)
    lanes = weight_in.shape[1]
    band, columns = start_state.shape[:2]
    start = lax.dynamic_slice_in_dim(start_state, core * 2 * lanes, 2 * lanes, 3)
    start = start.reshape(band, columns, 2, 2, lanes).transpose(3, 0, 1, 2, 4)
    start = jnp.where(chip == 0, start, jnp.float32(0.0)).reshape(2, band, columns, 2 * lanes)
    return layer(weight_in, weight_out, frames_in, start, log_decay, rotation, skip_gain)


def fits(frames_in, weight_in):
    count, band, columns, channels = frames_in.shape
    chips, cores, rows = (lax.axis_size(a) for a in (CHIPS, CORE, ROWS))
    return (
        (chips, rows) == (4, 2 * cores)
        and weight_in.shape[1] % 128 == 0
        and channels % 128 == 0
        and columns % 16 == 0
        and band >= 4
        and count % 4 == 0
    )


def on_device(frames_in, weight_in, weight_out, log_decay, rotation, start_state, skip_gain):
    if fits(frames_in, weight_in):
        return fused(frames_in, weight_in, weight_out, log_decay, rotation, start_state, skip_gain)
    frame_count, band_rows, columns, channels = frames_in.shape
    shard = weight_in.shape[1]
    chips, cores, rows = (lax.axis_size(a) for a in (CHIPS, CORE, ROWS))
    core, chip = lax.axis_index(CORE), lax.axis_index(CHIPS)
    half = shard // cores
    many = chips // 2
    piece = half // (2 * many)

    def own(vector, axis):
        picks = [
            jnp.concatenate(
                [
                    lax.slice_in_dim(vector, r * shard + c * half, r * shard + (c + 1) * half, axis=axis)
                    for r in range(rows)
                ],
                axis=axis,
            )
            for c in range(cores)
        ]
        return jnp.where(core == 0, picks[0], picks[1])

    states = rows * half
    slice_in = lax.dynamic_slice_in_dim(weight_in, core * half, half, 1)
    slice_out = lax.dynamic_slice_in_dim(weight_out, core * half, half, 2)
    own_in = slice_in.reshape(2, many, 2, piece, 9 * channels)
    own_out = slice_out.reshape(9, 2, many, 2, piece, channels)

    mine = with_halo(frames_in)
    theirs = swapped(mine)
    first = jnp.where(core == 0, mine, theirs)
    second = jnp.where(core == 0, theirs, mine)
    field = jnp.concatenate([first, second], axis=0)
    total = field.shape[0]

    if piece % 16 == 0 and total % GROUPS == 0:
        both, out_full = drive(own_in, own_out, field, chips, rows)
        both = both.reshape(total, band_rows, columns, 2 * states)
    else:
        in_full = spread(own_in, 0, chips, rows, 0).reshape(2, states, 3, 3, channels)
        out_full = spread(own_out, 1, chips, rows, 1)
        both = jnp.concatenate(
            [conv(field, in_full[part], "OHWI") for part in range(2)], axis=-1
        )

    log_rate, angle = own(log_decay, 0), own(rotation, 0)
    start = own(start_state, 3)
    lam_re, lam_im = powers(log_rate, angle, jnp.float32(1.0))
    begin = jnp.concatenate([start[:, :, 0], start[:, :, 1]], axis=-1)
    begin = jnp.where(chip == 0, begin, jnp.float32(0.0))
    factor = jnp.stack([lam_re, lam_im])
    tail = recur(both, begin, factor, True)
    carry_re = carry_im = jnp.float32(0.0)
    for step in range(1, chips):
        far = shifted(tail, CHIPS, step).astype(jnp.float32)
        jump_re, jump_im = powers(log_rate, angle, jnp.float32(total * (step - 1)))
        carry_re = carry_re + jump_re * far[..., :states] - jump_im * far[..., states:]
        carry_im = carry_im + jump_re * far[..., states:] + jump_im * far[..., :states]
    begin = begin + jnp.concatenate([carry_re, carry_im], axis=-1)
    held = with_halo(recur(both, begin, factor, False))

    out_weight = out_full.reshape(3, 3, 2 * states, channels)
    held_theirs = lax.dynamic_slice_in_dim(held, (1 - core) * frame_count, frame_count, 0)
    held_mine = lax.dynamic_slice_in_dim(held, core * frame_count, frame_count, 0)
    sent = conv(held_theirs, out_weight, "HWIO").astype(jnp.bfloat16)
    got = swapped(sent).astype(jnp.float32)
    mixing = conv(held_mine, out_weight, "HWIO") + got
    pre_act = mixing + skip_gain * frames_in.astype(jnp.float32)
    return jax.nn.gelu(pre_act, approximate=False).astype(jnp.bfloat16)


def solution(mesh):
    count, rows = mesh.devices.shape
    fine = Mesh(mesh.devices.reshape(count // 2, 2, rows), (CHIPS, CORE, ROWS))
    frames = P((CHIPS, CORE), ROWS, None, None)
    return jax.shard_map(
        on_device,
        mesh=fine,
        in_specs=(
            frames,
            P(None, ROWS, None),
            P(None, None, ROWS, None),
            P(),
            P(),
            P(ROWS, None, None, None),
            P(),
        ),
        out_specs=frames,
        check_vma=False,
    )
```

```python
import functools
import jax
import jax.numpy as jnp
from jax import lax
from jax.experimental import pallas as pl
from jax.experimental.pallas import tpu as pltpu
from jax.sharding import Mesh, PartitionSpec as P

CHIPS, CORE, ROWS = "chips", "core", "rows"


def shifted(value, axis, step):
    count = lax.axis_size(axis)
    pairs = [(i, i + step) for i in range(count) if 0 <= i + step < count]
    return lax.ppermute(value, axis, pairs)


def swapped(value):
    return lax.ppermute(value, CORE, [(0, 1), (1, 0)])


def with_halo(field):
    above = shifted(field[:, -1:], ROWS, 1)
    below = shifted(field[:, :1], ROWS, -1)
    return jnp.concatenate([above, field, below], axis=1)


def chip_at(place, chips):
    far = place // (chips // 2)
    return (1 - far) * (2 * place) + far * (2 * (chips - 1 - place) + 1)


def place_of(chip, chips):
    odd = chip % 2
    return (1 - odd) * (chip // 2) + odd * (chips - 1 - chip // 2)


def meet(chips, rows, chip, row, onward, back):
    barrier = pltpu.get_barrier_semaphore()

    def greet(**where):
        pl.semaphore_signal(
            barrier, inc=1, device_id=where, device_id_type=pl.DeviceIdType.MESH
        )

    greet(chips=onward)
    greet(chips=back)

    @pl.when(row > 0)
    def _():
        greet(rows=row - 1)

    @pl.when(row < rows - 1)
    def _():
        greet(rows=row + 1)

    sides = (row + rows - 1) // rows + (2 * rows - 2 - row) // rows
    pl.semaphore_wait(barrier, 2 + sides)


def spreader(leads, chips, rows, own_ref, full_ref, z_send, z_recv, r_send, r_recv, own_sem):
    chip, row = lax.axis_index(CHIPS), lax.axis_index(ROWS)
    place = place_of(chip, chips)
    onward = chip_at((place + 1) % chips, chips)
    back = chip_at((place + chips - 1) % chips, chips)
    many = chips // 2
    lead = (slice(None),) * leads

    def own_slice():
        return own_ref.at[lead + (chip // many, chip % many)]

    def block(shard, source, piece=None):
        at = lead + (source // many, shard, source % many)
        return full_ref.at[at if piece is None else at + (piece,)]

    keep = pltpu.make_async_copy(
        own_ref, full_ref.at[lead + (slice(None), row)], own_sem
    )

    def line(side, step):
        step_way = 1 - 2 * side
        shard = row - step_way * step
        src = own_slice() if step == 0 else block(shard, chip)
        return pltpu.make_async_remote_copy(
            src_ref=src,
            dst_ref=block(shard, chip),
            send_sem=z_send.at[side, step],
            recv_sem=z_recv.at[side, step],
            device_id={ROWS: row + step_way},
            device_id_type=pl.DeviceIdType.MESH,
        )

    def landed(side, step):
        shard = row - (1 - 2 * side) * (step + 1)
        here = block(shard, chip)
        return pltpu.make_async_remote_copy(
            src_ref=here,
            dst_ref=here,
            send_sem=z_send.at[side, step],
            recv_sem=z_recv.at[side, step],
            device_id={ROWS: row},
            device_id_type=pl.DeviceIdType.MESH,
        )

    def ring(side, step, way, turn):
        turn_way = 1 - 2 * way
        shard = row - (1 - 2 * side) * (step + 1)
        source = chip_at((place - turn_way * turn + chips) % chips, chips)
        here = block(shard, source, way)
        return pltpu.make_async_remote_copy(
            src_ref=here,
            dst_ref=here,
            send_sem=r_send.at[side, step, way, turn],
            recv_sem=r_recv.at[side, step, way, turn],
            device_id={CHIPS: back if way else onward},
            device_id_type=pl.DeviceIdType.MESH,
        )

    def ring_landed(side, step, way, turn):
        turn_way = 1 - 2 * way
        shard = row - (1 - 2 * side) * (step + 1)
        source = chip_at((place - turn_way * (turn + 1) + 2 * chips) % chips, chips)
        here = block(shard, source, way)
        return pltpu.make_async_remote_copy(
            src_ref=here,
            dst_ref=here,
            send_sem=r_send.at[side, step, way, turn],
            recv_sem=r_recv.at[side, step, way, turn],
            device_id={CHIPS: back if way else onward},
            device_id_type=pl.DeviceIdType.MESH,
        )

    def sends(side, step):
        near = row - step if side == 0 else rows - 1 - row - step
        room = rows - 1 - row if side == 0 else row
        return jnp.logical_and(near >= 0, room > 0)

    def comes(side, step):
        return (row if side == 0 else rows - 1 - row) > step

    def begin():
        keep.start()
        for side in range(2):

            @pl.when(sends(side, 0))
            def _():
                line(side, 0).start()

    def advance(tick):
        if tick < rows - 1:
            for side in range(2):

                @pl.when(comes(side, tick))
                def _():
                    landed(side, tick).wait_recv()
                    if tick + 1 < rows - 1:

                        @pl.when(sends(side, tick + 1))
                        def _():
                            line(side, tick + 1).start()

                    for way in range(2):
                        ring(side, tick, way, 0).start()

        for turn in range(1, chips):
            step = tick - turn
            if 0 <= step < rows - 1:
                for side in range(2):

                    @pl.when(comes(side, step))
                    def _():
                        for way in range(2):
                            ring_landed(side, step, way, turn - 1).wait_recv()
                            if turn < chips - 1:
                                ring(side, step, way, turn).start()

    def finish():
        for side in range(2):
            for step in range(rows - 1):

                @pl.when(sends(side, step))
                def _():
                    line(side, step).wait_send()

                @pl.when(comes(side, step))
                def _():
                    for way in range(2):
                        for turn in range(chips - 1):
                            ring(side, step, way, turn).wait_send()

    return begin, advance, finish, keep


def spread_kernel(leads, chips, rows, *refs):
    chip, row = lax.axis_index(CHIPS), lax.axis_index(ROWS)
    place = place_of(chip, chips)
    onward = chip_at((place + 1) % chips, chips)
    back = chip_at((place + chips - 1) % chips, chips)
    meet(chips, rows, chip, row, onward, back)
    begin, advance, finish, keep = spreader(leads, chips, rows, *refs)
    begin()
    for tick in range(rows - 1 + chips - 1):
        advance(tick)
    finish()
    keep.wait()


def semaphores(chips, rows):
    return [
        pltpu.SemaphoreType.DMA((2, rows - 1)),
        pltpu.SemaphoreType.DMA((2, rows - 1)),
        pltpu.SemaphoreType.DMA((2, rows - 1, 2, chips - 1)),
        pltpu.SemaphoreType.DMA((2, rows - 1, 2, chips - 1)),
        pltpu.SemaphoreType.DMA,
    ]


GROUPS = 4


def drive_kernel(chips, rows, in_ref, out_ref, field_ref, driven_ref, full_out, full_in, views, *sems):
    chip, row = lax.axis_index(CHIPS), lax.axis_index(ROWS)
    place = place_of(chip, chips)
    onward = chip_at((place + 1) % chips, chips)
    back = chip_at((place + chips - 1) % chips, chips)
    meet(chips, rows, chip, row, onward, back)
    count = len(sems) // 2
    first = spreader(0, chips, rows, in_ref, full_in, *sems[:count])
    second = spreader(1, chips, rows, out_ref, full_out, *sems[count:])
    ticks, delay = rows - 1 + chips - 1, rows - 1
    total, padded, columns, channels = field_ref.shape
    band = padded - 2
    group = total // GROUPS

    def compute(index):
        at = index * group
        taps = [
            views[b, at : at + group, a : a + band].reshape(group * band * columns, channels)
            for a in range(3)
            for b in range(3)
        ]
        window = jnp.concatenate(taps, axis=1)
        for part in range(2):
            weight = full_in[part]
            weight = weight.reshape(-1, weight.shape[-1])
            states = weight.shape[0]
            driven_ref[pl.ds(index * window.shape[0], window.shape[0]), part * states : (part + 1) * states] = (
                lax.dot_general(
                    window, weight, (((1,), (1,)), ((), ())), preferred_element_type=jnp.float32
                )
            )

    first[0]()

    @pl.loop(0, total)
    def _(frame):
        whole = field_ref[frame]
        wide = whole.astype(jnp.float32)
        edge = jnp.zeros((padded, 1, channels), jnp.float32)
        before = jnp.concatenate([edge, wide[:, : columns - 1]], axis=1)
        after = jnp.concatenate([wide[:, 1:], edge], axis=1)
        views[0, frame] = before.astype(whole.dtype)
        views[1, frame] = whole
        views[2, frame] = after.astype(whole.dtype)

    for tick in range(ticks):
        first[1](tick)
        if tick == delay - 1:
            second[0]()
        if tick >= delay:
            second[1](tick - delay)
    first[3].wait()
    for index in range(GROUPS):
        compute(index)
        if ticks - delay + index < ticks:
            second[1](ticks - delay + index)
    for tick in range(ticks - delay + GROUPS, ticks):
        second[1](tick)
    first[2]()
    second[2]()
    second[3].wait()


def drive(own_in, own_out, field, chips, rows):
    many_in = own_in.shape[:1] + (rows,) + own_in.shape[1:]
    many_out = own_out.shape[:2] + (rows,) + own_out.shape[2:]
    total, padded, columns, channels = field.shape
    pixels = total * (padded - 2) * columns
    states = many_in[1] * many_in[2] * many_in[3] * many_in[4]
    vmem = pl.BlockSpec(memory_space=pltpu.VMEM)
    return pl.pallas_call(
        functools.partial(drive_kernel, chips, rows),
        out_shape=(
            jax.ShapeDtypeStruct((pixels, 2 * states), jnp.float32),
            jax.ShapeDtypeStruct(many_out, own_out.dtype),
        ),
        in_specs=[vmem, vmem, vmem],
        out_specs=(vmem, pl.BlockSpec(memory_space=pl.ANY)),
        scratch_shapes=[
            pltpu.VMEM(many_in, own_in.dtype),
            pltpu.VMEM((3,) + field.shape, field.dtype),
        ]
        + semaphores(chips, rows)
        + semaphores(chips, rows),
        compiler_params=pltpu.CompilerParams(
            collective_id=2, has_side_effects=True, vmem_limit_bytes=60 * 1024 * 1024
        ),
    )(own_in, own_out, field)


def spread(own, leads, chips, rows, number):
    shape = own.shape[: leads + 1] + (rows,) + own.shape[leads + 1 :]
    any_space = pl.BlockSpec(memory_space=pl.ANY)
    return pl.pallas_call(
        functools.partial(spread_kernel, leads, chips, rows),
        out_shape=jax.ShapeDtypeStruct(shape, own.dtype),
        in_specs=[pl.BlockSpec(memory_space=pltpu.VMEM)],
        out_specs=any_space,
        scratch_shapes=semaphores(chips, rows),
        compiler_params=pltpu.CompilerParams(collective_id=number, has_side_effects=True),
    )(own)


def conv(field, weight, form):
    return lax.conv_general_dilated(
        field, weight, (1, 1), ((0, 0), (1, 1)),
        dimension_numbers=("NHWC", form, "NHWC"),
        preferred_element_type=jnp.float32,
    )


def recur_kernel(last_only, both_ref, begin_ref, factor_ref, result_ref):
    states = factor_ref.shape[1]
    lam_re, lam_im = factor_ref[0:1, :], factor_ref[1:2, :]
    state_re, state_im = begin_ref[0, :, :states], begin_ref[0, :, states:]
    total = both_ref.shape[0]
    for t in range(total):
        state_re, state_im = (
            lam_re * state_re - lam_im * state_im + both_ref[t, 0, :, :states],
            lam_re * state_im + lam_im * state_re + both_ref[t, 0, :, states:],
        )
        if not last_only:
            result_ref[t, 0, :, :states] = state_re.astype(result_ref.dtype)
            result_ref[t, 0, :, states:] = state_im.astype(result_ref.dtype)
    if last_only:
        result_ref[0, :, :states] = state_re.astype(result_ref.dtype)
        result_ref[0, :, states:] = state_im.astype(result_ref.dtype)


def recur(both, begin, factor, last_only):
    total, band, columns, lanes = both.shape
    frames = pl.BlockSpec((total, 1, columns, lanes), lambda i: (0, i, 0, 0))
    single = pl.BlockSpec((1, columns, lanes), lambda i: (i, 0, 0))
    shape = both.shape[1:] if last_only else both.shape
    return pl.pallas_call(
        functools.partial(recur_kernel, last_only),
        out_shape=jax.ShapeDtypeStruct(shape, jnp.bfloat16),
        grid=(band,),
        in_specs=[frames, single, pl.BlockSpec(factor.shape, lambda i: (0, 0))],
        out_specs=single if last_only else frames,
    )(both, begin, factor)


def powers(log_rate, angle, exponent):
    modulus = jnp.exp(-log_rate * exponent)
    return modulus * jnp.cos(angle * exponent), modulus * jnp.sin(angle * exponent)


ORDER = (1, 0, 2)


def power(re, im, exponent):
    out_re, out_im = jnp.ones_like(re), jnp.zeros_like(im)
    while exponent:
        if exponent % 2:
            out_re, out_im = out_re * re - out_im * im, out_re * im + out_im * re
        re, im = re * re - im * im, 2.0 * (re * im)
        exponent //= 2
    return out_re, out_im


def layer_kernel(
    win, wout, frames, start, rate, angle, skip, out,
    started, begin, views, full_in, full_out, driven, held, acc, tail, tail_half, met, joint, far_joint, given, got,
    z_send, z_recv, x_send, x_recv, y_send, y_recv,
    halo_send, halo_recv, pass_send, pass_recv, edge_send, edge_recv,
    first_send, first_recv, second_send, second_recv, swap_send, swap_recv, part_send, part_recv, local,
):
    chip, core, row = (lax.axis_index(a) for a in (CHIPS, CORE, ROWS))
    rows = lax.axis_size(ROWS)
    other = 1 - core
    beside = chip + 1 - 2 * (chip % 2)
    across = (chip + 2) % 4
    opposite = 3 - chip
    _, many, padded, columns, channels = views.shape
    band, mine = padded - 2, many // 2
    lanes = tail.shape[-1] // 2
    depth = 3 * channels
    near = row // 2
    slots = (near, 1 - near)
    turns = (row + 1 - 2 * (row % 2), 2 - near, 3 * (1 - near))
    here = pl.multiple_of(core * mine, mine)
    there = pl.multiple_of(other * mine, mine)
    has_up, has_down = row > 0, row < rows - 1

    def remote(src, dst, send, recv, **where):
        return pltpu.make_async_remote_copy(
            src_ref=src, dst_ref=dst, send_sem=send, recv_sem=recv,
            device_id=where, device_id_type=pl.DeviceIdType.MESH,
        )

    def block(w, shard, quarter, o):
        a, pair, j = ORDER[o], shard // 2, shard % 2
        if w == 0:
            return full_in.at[pair, :, j, quarter, :, a * depth : (a + 1) * depth]
        return full_out.at[a, :, pair, :, j, quarter]

    def source(w, quarter, o):
        a = ORDER[o]
        if w == 0:
            return win.at[:, core, quarter, :, a * depth : (a + 1) * depth]
        return wout.at[a, :, :, core, quarter]

    def z_copy(w, shard, k, kind, first, to):
        quarter, o = (chip, k) if k < 3 else (opposite, 2)
        dst = block(w, shard, quarter, o)
        src = source(w, quarter, o) if first else dst
        return remote(src, dst, z_send.at[w, kind, k], z_recv.at[w, shard, k], **{ROWS: to})

    def x_copy(w, turn, i):
        quarter, o = (chip, i) if i < 3 else (across, 1)
        ref = block(w, turns[turn], quarter, o)
        return remote(ref, ref, x_send.at[w, turn, i], x_recv.at[w, turn, i], **{CHIPS: beside})

    def y_copy(w, turn, i):
        quarter, o = (chip, i) if i < 3 else (beside, 0)
        ref = block(w, turns[turn], quarter, o)
        return remote(ref, ref, y_send.at[w, turn, i], y_recv.at[w, turn, i], **{CHIPS: across})

    def x_came(w, turn, i):
        quarter, o = (beside, i) if i < 3 else (opposite, 1)
        ref = block(w, turns[turn], quarter, o)
        remote(ref, ref, x_send.at[w, turn, i], x_recv.at[w, turn, i], **{CHIPS: beside}).wait_recv()

    def y_came(w, turn, i):
        quarter, o = (across, i) if i < 3 else (opposite, 0)
        ref = block(w, turns[turn], quarter, o)
        remote(ref, ref, y_send.at[w, turn, i], y_recv.at[w, turn, i], **{CHIPS: across}).wait_recv()

    def relays(turn):
        below = turns[turn] > row
        return jnp.logical_and(below, has_up), jnp.logical_and(jnp.logical_not(below), has_down)

    inner = jnp.logical_and(has_up, has_down)
    mate_up = row % 2 == 1
    early_up = jnp.logical_and(has_up, jnp.logical_or(jnp.logical_not(inner), jnp.logical_not(mate_up)))
    early_down = jnp.logical_and(has_down, jnp.logical_or(jnp.logical_not(inner), mate_up))

    def send_own(w, ks, up=has_up, down=has_down):
        for k in ks:
            @pl.when(up)
            def _():
                z_copy(w, row, k, 3, True, row - 1).start()

            @pl.when(down)
            def _():
                z_copy(w, row, k, 4, True, row + 1).start()

    late_up = jnp.logical_and(has_up, jnp.logical_not(early_up))
    late_down = jnp.logical_and(has_down, jnp.logical_not(early_down))

    def send_early(w):
        send_own(w, range(4), early_up, early_down)

    def send_late(w, which):
        send_own(
            w, range(4), jnp.logical_and(late_up, core == which), jnp.logical_and(late_down, core == which)
        )

    def bring(w, turn, k):
        shard = turns[turn]
        z_copy(w, shard, k, turn, False, row).wait_recv()
        up, down = relays(turn)

        @pl.when(up)
        def _():
            z_copy(w, shard, k, turn, False, row - 1).start()

        @pl.when(down)
        def _():
            z_copy(w, shard, k, turn, False, row + 1).start()

    def fan(w, turn, k, x=True, y=True):
        if x:
            x_copy(w, turn, k).start()
        if y:
            y_copy(w, turn, k).start()

    def z_event(w, turn, k):
        bring(w, turn, k)
        if k < 3:
            fan(w, turn, k)

    def x_event(w, turn):
        x_came(w, turn, 0)
        y_copy(w, turn, 3).start()

    def y_event(w, turn):
        y_came(w, turn, 1)
        x_copy(w, turn, 3).start()

    def events(w, turn):
        return [
            functools.partial(z_event, w, turn, 0),
            functools.partial(z_event, w, turn, 1),
            functools.partial(x_event, w, turn),
            functools.partial(z_event, w, turn, 2),
            functools.partial(y_event, w, turn),
            functools.partial(z_event, w, turn, 3),
        ]

    def came(w, turn, o):
        if o != 0:
            x_came(w, turn, o)
        else:
            y_came(w, turn, 3)
        if o != 1:
            y_came(w, turn, o)
        else:
            x_came(w, turn, 3)

    def complete(w, rank, o):
        for turn in ((1, 2) if rank else (0,)):
            came(w, turn, o)

    def settle(w):
        for k in range(4):
            @pl.when(has_up)
            def _():
                z_copy(w, row, k, 3, True, row - 1).wait_send()

            @pl.when(has_down)
            def _():
                z_copy(w, row, k, 4, True, row + 1).wait_send()

            for turn in range(3):
                up, down = relays(turn)

                @pl.when(jnp.logical_or(up, down))
                def _():
                    z_copy(w, turns[turn], k, turn, False, row).wait_send()

        for turn in range(3):
            for i in range(4):
                x_copy(w, turn, i).wait_send()
                y_copy(w, turn, i).wait_send()

    barrier = pltpu.get_barrier_semaphore()

    def greet(**where):
        pl.semaphore_signal(barrier, inc=1, device_id=where, device_id_type=pl.DeviceIdType.MESH)

    greet(**{CORE: other})
    greet(**{CHIPS: beside})
    greet(**{CHIPS: across})

    @pl.when(has_up)
    def _():
        greet(**{ROWS: row - 1})

    @pl.when(has_down)
    def _():
        greet(**{ROWS: row + 1})

    pl.semaphore_wait(barrier, 3 + (row + rows - 1) // rows + (2 * rows - 2 - row) // rows)

    mine_in = views.at[1, pl.ds(here, mine), 1 : band + 1]
    keep = pltpu.make_async_copy(frames, mine_in, local.at[0])
    hold_in = pltpu.make_async_copy(win.at[:, core], full_in.at[near, :, row % 2], local.at[1])
    hold_out = pltpu.make_async_copy(wout.at[:, :, :, core], full_out.at[:, :, near, :, row % 2], local.at[2])
    hold_start = pltpu.make_async_copy(start, started, local.at[3])
    swap = remote(frames, mine_in, swap_send, swap_recv, **{CORE: other})
    theirs_in = views.at[1, pl.ds(there, mine), 1 : band + 1]

    def halo(side, start):
        at = views.at[1, pl.ds(here, mine), band + 1 if side == 0 else 0]
        src = frames.at[:, 0 if side == 0 else band - 1]
        return remote(src, at, halo_send.at[side], halo_recv.at[side], **{ROWS: row - 1 if side == 0 else row + 1})

    def halo_at(side, first):
        return views.at[1, pl.ds(first, mine), band + 1 if side == 0 else 0]

    def halo_came(side):
        ref = halo_at(side, here)
        remote(ref, ref, halo_send.at[side], halo_recv.at[side], **{ROWS: row}).wait_recv()

    def handed(side, first):
        ref = halo_at(side, first)
        return remote(ref, ref, pass_send.at[side], pass_recv.at[side], **{CORE: other})

    gives = (has_up, has_down)
    takes = (has_down, has_up)

    send_own(0, range(4))
    for side in range(2):
        @pl.when(gives[side])
        def _():
            halo(side, True).start()

    swap.start()
    keep.start()

    hold_in.start()
    hold_out.start()

    @pl.when(chip == 0)
    def _():
        hold_start.start()

    blank = jnp.zeros((columns, channels), views.dtype)
    for side in range(2):
        edge = band + 1 if side == 0 else 0

        @pl.when(jnp.logical_not(takes[side]))
        def _():
            @pl.loop(0, many)
            def _(f):
                views[1, f, edge] = blank
                for slot in range(2):
                    held[slot, 1, f, edge] = blank[:, : 2 * lanes]

    place = lax.broadcasted_iota(jnp.int32, (columns, 1), 0)
    not_first, not_last = place > 0, place < columns - 1

    def sides(wide):
        before = jnp.where(not_first, pltpu.roll(wide, 1, 0), 0.0)
        after = jnp.where(not_last, pltpu.roll(wide, columns - 1, 0), 0.0)
        return before.astype(views.dtype), after.astype(views.dtype)

    def spread_views(first):
        @pl.loop(0, mine)
        def _(i):
            f = first + i

            @pl.loop(1, band + 1)
            def _(r):
                views[0, f, r], views[2, f, r] = sides(views[1, f, r].astype(jnp.float32))

    def spread_edges(first):
        @pl.loop(0, mine)
        def _(i):
            f = first + i
            for r in (0, band + 1):
                views[0, f, r], views[2, f, r] = sides(views[1, f, r].astype(jnp.float32))

    def hand_over():
        for side in range(2):
            @pl.when(takes[side])
            def _():
                halo_came(side)
                handed(side, here).start()

        spread_edges(here)

    def take_over():
        for side in range(2):
            @pl.when(takes[side])
            def _():
                handed(side, there).wait_recv()

        spread_edges(there)

    def drive(rank, o, m0, m1):
        slot, a = slots[rank], ORDER[o]

        @pl.loop(m0, m1)
        def _(m):
            at = pl.ds(m * 2, 2)
            pixels = 2 * band * columns
            window = jnp.concatenate(
                [views[b, at, a : a + band].reshape(pixels, channels) for b in range(3)], axis=1
            )
            weight = full_in[slot, :, :, :, :, a * depth : (a + 1) * depth].reshape(2 * lanes, depth)
            result = lax.dot_general(
                window, weight, (((1,), (1,)), ((), ())), preferred_element_type=jnp.float32
            ).reshape(2, band, columns, 2 * lanes)
            if o == 0:
                driven[slot, at] = result
            else:
                driven[slot, at] += result

    blocks = many // 2

    low = lax.broadcasted_iota(jnp.int32, (1, lanes), 1) < lanes // 2

    def joined(first, second):
        first = jnp.where(core == 0, first, pltpu.roll(first, lanes // 2, 1))
        second = jnp.where(core == 0, pltpu.roll(second, lanes // 2, 1), second)
        return jnp.where(low, first, second)

    def factors(rank):
        def lane_row(ref):
            first, second = (
                jnp.broadcast_to(ref[pl.ds(2 * slots[rank] + j, 1), :], (8, lanes)) for j in range(2)
            )
            return joined(first, second)[:1]

        modulus, turn = jnp.exp(-lane_row(rate)), lane_row(angle)
        return modulus * jnp.cos(turn), modulus * jnp.sin(turn)

    def prepare():
        @pl.when(chip == 0)
        def _():
            hold_start.wait()

            @pl.loop(0, band)
            def _(r):
                for pair in range(2):
                    for part in range(2):
                        at = slice(part * lanes, (part + 1) * lanes)
                        begin[pair, r, :, at] = joined(
                            started[r, :, 4 * pair + part], started[r, :, 4 * pair + 2 + part]
                        )

        @pl.when(chip > 0)
        def _():
            @pl.loop(0, band)
            def _(r):
                for pair in range(2):
                    begin[pair, r] = jnp.zeros((columns, 2 * lanes), jnp.float32)

    def ends(rank):
        slot = slots[rank]
        lam_re, lam_im = factors(rank)

        @pl.loop(0, band)
        def _(r):
            re, im = begin[slot, r, :, :lanes], begin[slot, r, :, lanes:]
            for t in range(many):
                re, im = (
                    lam_re * re - lam_im * im + driven[slot, t, r, :, :lanes],
                    lam_re * im + lam_im * re + driven[slot, t, r, :, lanes:],
                )
            tail[slot, r, :, :lanes] = re
            tail[slot, r, :, lanes:] = im
            tail_half[slot, r, :, :lanes] = re.astype(tail_half.dtype)
            tail_half[slot, r, :, lanes:] = im.astype(tail_half.dtype)

    tells, hears = chip < 3, chip != 2
    joins = chip < 2

    def first_copy(rank):
        slot = slots[rank]
        return remote(
            tail_half.at[slot], met.at[slot], first_send.at[rank], first_recv.at[rank], **{CHIPS: beside}
        )

    def second_copy(rank):
        slot = slots[rank]
        return remote(
            joint.at[slot], far_joint.at[slot], second_send.at[rank], second_recv.at[rank], **{CHIPS: across}
        )

    def tell(rank):
        @pl.when(tells)
        def _():
            first_copy(rank).start()

    def merge(rank):
        slot = slots[rank]
        lam_re, lam_im = factors(rank)
        jump_re, jump_im = power(lam_re, lam_im, many)

        def combine(r, late_re, late_im, early_re, early_im):
            return (
                late_re + jump_re * early_re - jump_im * early_im,
                late_im + jump_re * early_im + jump_im * early_re,
            )

        def split(ref, r):
            return ref[slot, r, :, :lanes].astype(jnp.float32), ref[slot, r, :, lanes:].astype(jnp.float32)

        def put(ref, r, value):
            ref[slot, r, :, :lanes] = value[0].astype(ref.dtype)
            ref[slot, r, :, lanes:] = value[1].astype(ref.dtype)

        @pl.when(hears)
        def _():
            first_copy(rank).wait_recv()

        @pl.when(chip == 0)
        def _():
            @pl.loop(0, band)
            def _(r):
                put(joint, r, combine(r, *split(met, r), *split(tail, r)))
                put(tail, r, split(begin, r))

        @pl.when(chip == 1)
        def _():
            @pl.loop(0, band)
            def _(r):
                put(joint, r, combine(r, *split(tail, r), *split(met, r)))
                put(tail, r, split(met, r))

        @pl.when(joins)
        def _():
            second_copy(rank).start()

    def carry(rank):
        slot = slots[rank]
        lam_re, lam_im = factors(rank)
        jump_re, jump_im = power(lam_re, lam_im, many)

        @pl.when(jnp.logical_not(joins))
        def _():
            second_copy(rank).wait_recv()

        @pl.when(chip == 2)
        def _():
            @pl.loop(0, band)
            def _(r):
                tail[slot, r] = far_joint[slot, r].astype(jnp.float32)

        @pl.when(chip == 3)
        def _():
            @pl.loop(0, band)
            def _(r):
                late, early = met[slot, r].astype(jnp.float32), far_joint[slot, r].astype(jnp.float32)
                re, im = early[:, :lanes], early[:, lanes:]
                tail[slot, r, :, :lanes] = late[:, :lanes] + jump_re * re - jump_im * im
                tail[slot, r, :, lanes:] = late[:, lanes:] + jump_re * im + jump_im * re

    def scan_rows(rank, start, count, stride):
        slot = slots[rank]
        lam_re, lam_im = factors(rank)

        @pl.loop(0, count)
        def _(i):
            r = start + i * stride
            re, im = tail[slot, r, :, :lanes], tail[slot, r, :, lanes:]
            for t in range(many):
                re, im = (
                    lam_re * re - lam_im * im + driven[slot, t, r, :, :lanes],
                    lam_re * im + lam_im * re + driven[slot, t, r, :, lanes:],
                )
                for part, value in enumerate((re, im)):
                    at = slice(part * lanes, (part + 1) * lanes)
                    before, after = sides(value)
                    held[slot, 0, t, 1 + r, :, at] = before
                    held[slot, 1, t, 1 + r, :, at] = value.astype(held.dtype)
                    held[slot, 2, t, 1 + r, :, at] = after

    def edge_copy(rank, side):
        slot = slots[rank]
        return remote(
            held.at[slot, 1, :, 1 if side == 0 else band],
            held.at[slot, 1, :, band + 1 if side == 0 else 0],
            edge_send.at[rank, side],
            edge_recv.at[slot, side],
            **{ROWS: row - 1 if side == 0 else row + 1},
        )

    def scan(rank):
        scan_rows(rank, 0, 2, band - 1)
        scan_rows(rank, 1, (band - 2) // 2, 1)
        for side in range(2):
            @pl.when(gives[side])
            def _():
                edge_copy(rank, side).start()
        scan_rows(rank, 1 + (band - 2) // 2, band - 2 - (band - 2) // 2, 1)

    def edges_came(rank):
        slot = slots[rank]
        for side in range(2):
            at = band + 1 if side == 0 else 0
            ref = held.at[slot, 1, :, at]

            @pl.when(takes[side])
            def _():
                remote(
                    ref, ref, edge_send.at[rank, side], edge_recv.at[slot, side], **{ROWS: row}
                ).wait_recv()

            @pl.loop(0, many)
            def _(f):
                held[slot, 0, f, at], held[slot, 2, f, at] = sides(held[slot, 1, f, at].astype(jnp.float32))

    def mix_block(rank, rights, first, fresh):
        slot = slots[rank]
        pixels = 2 * band * columns
        window = jnp.concatenate(
            [
                held[slot, b, pl.ds(first, 2), a : a + band].reshape(pixels, 2 * lanes)
                for a in rights
                for b in range(3)
            ],
            axis=1,
        )
        weight = jnp.concatenate([full_out[a, :, slot].reshape(6 * lanes, channels) for a in rights], axis=0)
        result = jnp.dot(window, weight, preferred_element_type=jnp.float32)
        result = result.reshape(2, band, columns, channels)
        if fresh:
            return result
        return acc[pl.ds(first, 2)] + result

    def mix(rank, rights, fresh, m0=0, m1=None):
        @pl.loop(m0, blocks if m1 is None else m1)
        def _(m):
            acc[pl.ds(m * 2, 2)] = mix_block(rank, rights, m * 2, fresh)

    def part_copy(m):
        at = pl.ds(m * 2, 2)
        return remote(
            given.at[at], got.at[at], part_send.at[m], part_recv.at[m], **{CORE: other}
        )

    def mix_last(rank, rights):
        for m in range(blocks // 2):
            given[m * 2 : m * 2 + 2] = mix_block(rank, rights, there + m * 2, False).astype(given.dtype)
            part_copy(m).start()
        for m in range(blocks // 2):
            acc[pl.ds(here + m * 2, 2)] = mix_block(rank, rights, here + m * 2, False)
        for m in range(blocks // 2):
            part_copy(m).wait_recv()

            @pl.loop(0, 2)
            def _(i):
                f = m * 2 + i

                @pl.loop(0, band)
                def _(r):
                    value = acc[here + f, r] + got[f, r].astype(jnp.float32)
                    value = value + skip[...] * views[1, here + f, 1 + r].astype(jnp.float32)
                    out[f, r] = (0.5 * value * (1.0 + lax.erf(value * 0.7071067811865476))).astype(out.dtype)

    steps = iter(events(0, 0))
    next(steps)()
    next(steps)()
    keep.wait()
    spread_views(here)
    next(steps)()
    next(steps)()
    prepare()
    next(steps)()
    next(steps)()
    remote(theirs_in, theirs_in, swap_send, swap_recv, **{CORE: other}).wait_recv()
    spread_views(there)
    hand_over()
    hold_in.wait()
    hold_out.wait()
    half = blocks // 2

    @pl.when(inner)
    def _():
        z_event(0, 1, 0)
        z_event(0, 1, 1)
        complete(0, 0, 0)
        drive(0, 0, 0, half)
        z_event(0, 1, 2)
        z_event(0, 1, 3)
        drive(0, 0, half, blocks)
        z_event(0, 2, 0)
        x_event(0, 1)
        take_over()
        complete(0, 0, 1)
        drive(0, 1, 0, half)
        z_event(0, 2, 1)
        y_event(0, 1)
        drive(0, 1, half, blocks)
        z_event(0, 2, 2)
        z_event(0, 2, 3)
        send_early(1)
        send_late(1, 0)
        complete(0, 0, 2)
        drive(0, 2, 0, blocks)
        ends(0)
        tell(0)
        x_event(0, 2)
        y_event(0, 2)
        complete(0, 1, 0)
        drive(1, 0, 0, blocks)
        send_late(1, 1)
        bring(1, 0, 0)
        bring(1, 0, 1)
        complete(0, 1, 1)
        merge(0)
        drive(1, 1, 0, blocks)
        bring(1, 0, 2)
        bring(1, 0, 3)
        fan(1, 0, 0)
        complete(0, 1, 2)
        drive(1, 2, 0, blocks)
        ends(1)
        tell(1)
        bring(1, 1, 0)
        bring(1, 1, 1)
        bring(1, 1, 2)
        bring(1, 1, 3)
        fan(1, 0, 1)
        carry(0)
        scan(0)
        bring(1, 2, 0)
        bring(1, 2, 1)
        merge(1)
        fan(1, 0, 2)
        x_event(1, 0)
        fan(1, 1, 0)
        y_event(1, 0)
        fan(1, 1, 1)
        bring(1, 2, 2)
        bring(1, 2, 3)
        fan(1, 1, 2)
        carry(1)
        scan(1)
        complete(1, 0, 0)
        mix(0, (1,), True)
        x_event(1, 1)
        fan(1, 2, 0)
        edges_came(0)
        complete(1, 0, 1)
        mix(0, (0,), False)
        y_event(1, 1)
        fan(1, 2, 1)
        fan(1, 2, 2)
        complete(1, 0, 2)
        mix(0, (2,), False)
        x_event(1, 2)
        y_event(1, 2)
        edges_came(1)
        complete(1, 1, 2)
        mix(1, (2,), False)
        complete(1, 1, 0)
        mix(1, (1,), False)
        complete(1, 1, 1)

    @pl.when(jnp.logical_not(inner))
    def _():
        z_event(0, 1, 0)
        complete(0, 0, 0)
        drive(0, 0, 0, half)
        z_event(0, 1, 1)
        drive(0, 0, half, blocks)
        x_event(0, 1)
        take_over()
        complete(0, 0, 1)
        drive(0, 1, 0, half)
        z_event(0, 1, 2)
        send_early(1)
        drive(0, 1, half, blocks)
        y_event(0, 1)
        z_event(0, 1, 3)
        complete(0, 0, 2)
        drive(0, 2, 0, half)
        z_event(0, 2, 0)
        drive(0, 2, half, blocks)
        z_event(0, 2, 1)
        ends(0)
        tell(0)
        x_event(0, 2)
        z_event(0, 2, 2)
        y_event(0, 2)
        complete(0, 1, 0)
        drive(1, 0, 0, blocks)
        z_event(0, 2, 3)
        complete(0, 1, 1)
        merge(0)
        drive(1, 1, 0, blocks)
        bring(1, 0, 0)
        fan(1, 0, 0)
        complete(0, 1, 2)
        drive(1, 2, 0, blocks)
        ends(1)
        tell(1)
        bring(1, 0, 1)
        fan(1, 0, 1)
        carry(0)
        scan(0)
        bring(1, 0, 2)
        fan(1, 0, 2, x=False)
        merge(1)
        fan(1, 0, 2, y=False)
        x_event(1, 0)
        bring(1, 0, 3)
        z_event(1, 1, 0)
        y_event(1, 0)
        z_event(1, 1, 1)
        carry(1)
        scan(1)
        z_event(1, 1, 2)
        complete(1, 0, 0)
        mix(0, (1,), True, 0, half)
        x_event(1, 1)
        mix(0, (1,), True, half)
        z_event(1, 1, 3)
        z_event(1, 2, 0)
        edges_came(0)
        complete(1, 0, 1)
        mix(0, (0,), False, 0, half)
        z_event(1, 2, 1)
        y_event(1, 1)
        mix(0, (0,), False, half)
        z_event(1, 2, 2)
        complete(1, 0, 2)
        mix(0, (2,), False, 0, half)
        x_event(1, 2)
        mix(0, (2,), False, half)
        z_event(1, 2, 3)
        y_event(1, 2)
        edges_came(1)
        complete(1, 1, 2)
        mix(1, (2,), False)
        complete(1, 1, 0)
        mix(1, (1,), False)
        complete(1, 1, 1)

    mix_last(1, (0,))
    settle(0)
    settle(1)
    swap.wait_send()
    for side in range(2):
        @pl.when(gives[side])
        def _():
            halo(side, False).wait_send()
            for rank in range(2):
                edge_copy(rank, side).wait_send()

        @pl.when(takes[side])
        def _():
            handed(side, here).wait_send()

    for rank in range(2):
        @pl.when(tells)
        def _():
            first_copy(rank).wait_send()

        @pl.when(joins)
        def _():
            second_copy(rank).wait_send()

    for m in range(blocks // 2):
        part_copy(m).wait_send()


def layer(weight_in, weight_out, frames_in, start, log_decay, rotation, skip_gain):
    count, band, columns, channels = frames_in.shape
    lanes = weight_in.shape[1]
    quarter = lanes // 8
    many = 2 * count
    vmem, anywhere = pl.BlockSpec(memory_space=pltpu.VMEM), pl.BlockSpec(memory_space=pl.ANY)
    dma = pltpu.SemaphoreType.DMA
    half = frames_in.dtype
    full = jnp.float32
    return pl.pallas_call(
        layer_kernel,
        out_shape=jax.ShapeDtypeStruct(frames_in.shape, half),
        in_specs=[anywhere, anywhere, anywhere, anywhere, vmem, vmem, vmem],
        out_specs=vmem,
        scratch_shapes=[
            pltpu.VMEM(start.shape, full),
            pltpu.VMEM((2, band, columns, 2 * lanes), full),
            pltpu.VMEM((3, many, band + 2, columns, channels), half),
            pltpu.VMEM((2, 2, 2, 4, quarter, 9 * channels), half),
            pltpu.VMEM((3, 3, 2, 2, 2, 4, quarter, channels), half),
            pltpu.VMEM((2, many, band, columns, 2 * lanes), full),
            pltpu.VMEM((2, 3, many, band + 2, columns, 2 * lanes), half),
            pltpu.VMEM((many, band, columns, channels), full),
            pltpu.VMEM((2, band, columns, 2 * lanes), full),
            pltpu.VMEM((2, band, columns, 2 * lanes), half),
            pltpu.VMEM((2, band, columns, 2 * lanes), half),
            pltpu.VMEM((2, band, columns, 2 * lanes), half),
            pltpu.VMEM((2, band, columns, 2 * lanes), half),
            pltpu.VMEM((count, band, columns, channels), half),
            pltpu.VMEM((count, band, columns, channels), half),
            dma((2, 5, 4)), dma((2, 4, 4)), dma((2, 3, 4)), dma((2, 3, 4)), dma((2, 3, 4)), dma((2, 3, 4)),
            dma((2,)), dma((2,)), dma((2,)), dma((2,)), dma((2, 2)), dma((2, 2)),
            dma((2,)), dma((2,)), dma((2,)), dma((2,)), dma, dma,
            dma((many // 4,)), dma((many // 4,)), dma((4,)),
        ],
        compiler_params=pltpu.CompilerParams(
            collective_id=3, has_side_effects=True, vmem_limit_bytes=63 * 1024 * 1024
        ),
    )(
        weight_in.reshape(2, 2, 4, quarter, 9 * channels),
        weight_out.reshape(3, 3, 2, 2, 4, quarter, channels),
        frames_in,
        start,
        log_decay.reshape(-1, lanes),
        rotation.reshape(-1, lanes),
        skip_gain.reshape(1, channels),
    )


def fused(frames_in, weight_in, weight_out, log_decay, rotation, start_state, skip_gain):
    lanes = weight_in.shape[1]
    band, columns = start_state.shape[:2]
    start = start_state.reshape(band, columns, 2, -1, lanes).swapaxes(2, 3).reshape(band, columns, -1, lanes)
    return layer(weight_in, weight_out, frames_in, start, log_decay, rotation, skip_gain)


def fits(frames_in, weight_in):
    count, band, columns, channels = frames_in.shape
    chips, cores, rows = (lax.axis_size(a) for a in (CHIPS, CORE, ROWS))
    return (
        (chips, rows) == (4, 2 * cores)
        and weight_in.shape[1] % 128 == 0
        and channels % 128 == 0
        and columns % 16 == 0
        and band >= 4
        and count % 4 == 0
    )


def on_device(frames_in, weight_in, weight_out, log_decay, rotation, start_state, skip_gain):
    if fits(frames_in, weight_in):
        return fused(frames_in, weight_in, weight_out, log_decay, rotation, start_state, skip_gain)
    frame_count, band_rows, columns, channels = frames_in.shape
    shard = weight_in.shape[1]
    chips, cores, rows = (lax.axis_size(a) for a in (CHIPS, CORE, ROWS))
    core, chip = lax.axis_index(CORE), lax.axis_index(CHIPS)
    half = shard // cores
    many = chips // 2
    piece = half // (2 * many)

    def own(vector, axis):
        picks = [
            jnp.concatenate(
                [
                    lax.slice_in_dim(vector, r * shard + c * half, r * shard + (c + 1) * half, axis=axis)
                    for r in range(rows)
                ],
                axis=axis,
            )
            for c in range(cores)
        ]
        return jnp.where(core == 0, picks[0], picks[1])

    states = rows * half
    slice_in = lax.dynamic_slice_in_dim(weight_in, core * half, half, 1)
    slice_out = lax.dynamic_slice_in_dim(weight_out, core * half, half, 2)
    own_in = slice_in.reshape(2, many, 2, piece, 9 * channels)
    own_out = slice_out.reshape(9, 2, many, 2, piece, channels)

    mine = with_halo(frames_in)
    theirs = swapped(mine)
    first = jnp.where(core == 0, mine, theirs)
    second = jnp.where(core == 0, theirs, mine)
    field = jnp.concatenate([first, second], axis=0)
    total = field.shape[0]

    if piece % 16 == 0 and total % GROUPS == 0:
        both, out_full = drive(own_in, own_out, field, chips, rows)
        both = both.reshape(total, band_rows, columns, 2 * states)
    else:
        in_full = spread(own_in, 0, chips, rows, 0).reshape(2, states, 3, 3, channels)
        out_full = spread(own_out, 1, chips, rows, 1)
        both = jnp.concatenate(
            [conv(field, in_full[part], "OHWI") for part in range(2)], axis=-1
        )

    log_rate, angle = own(log_decay, 0), own(rotation, 0)
    start = own(start_state, 3)
    lam_re, lam_im = powers(log_rate, angle, jnp.float32(1.0))
    begin = jnp.concatenate([start[:, :, 0], start[:, :, 1]], axis=-1)
    begin = jnp.where(chip == 0, begin, jnp.float32(0.0))
    factor = jnp.stack([lam_re, lam_im])
    tail = recur(both, begin, factor, True)
    carry_re = carry_im = jnp.float32(0.0)
    for step in range(1, chips):
        far = shifted(tail, CHIPS, step).astype(jnp.float32)
        jump_re, jump_im = powers(log_rate, angle, jnp.float32(total * (step - 1)))
        carry_re = carry_re + jump_re * far[..., :states] - jump_im * far[..., states:]
        carry_im = carry_im + jump_re * far[..., states:] + jump_im * far[..., :states]
    begin = begin + jnp.concatenate([carry_re, carry_im], axis=-1)
    held = with_halo(recur(both, begin, factor, False))

    out_weight = out_full.reshape(3, 3, 2 * states, channels)
    held_theirs = lax.dynamic_slice_in_dim(held, (1 - core) * frame_count, frame_count, 0)
    held_mine = lax.dynamic_slice_in_dim(held, core * frame_count, frame_count, 0)
    sent = conv(held_theirs, out_weight, "HWIO").astype(jnp.bfloat16)
    got = swapped(sent).astype(jnp.float32)
    mixing = conv(held_mine, out_weight, "HWIO") + got
    pre_act = mixing + skip_gain * frames_in.astype(jnp.float32)
    return jax.nn.gelu(pre_act, approximate=False).astype(jnp.bfloat16)


def solution(mesh):
    count, rows = mesh.devices.shape
    fine = Mesh(mesh.devices.reshape(count // 2, 2, rows), (CHIPS, CORE, ROWS))
    frames = P((CHIPS, CORE), ROWS, None, None)
    return jax.shard_map(
        on_device,
        mesh=fine,
        in_specs=(
            frames,
            P(None, ROWS, None),
            P(None, None, ROWS, None),
            P(),
            P(),
            P(ROWS, None, None, None),
            P(),
        ),
        out_specs=frames,
        check_vma=False,
    )
```

```python
import functools
import jax
import jax.numpy as jnp
from jax import lax
from jax.experimental import pallas as pl
from jax.experimental.pallas import tpu as pltpu
from jax.sharding import Mesh, PartitionSpec as P

CHIPS, CORE, ROWS = "chips", "core", "rows"


def shifted(value, axis, step):
    count = lax.axis_size(axis)
    pairs = [(i, i + step) for i in range(count) if 0 <= i + step < count]
    return lax.ppermute(value, axis, pairs)


def swapped(value):
    return lax.ppermute(value, CORE, [(0, 1), (1, 0)])


def with_halo(field):
    above = shifted(field[:, -1:], ROWS, 1)
    below = shifted(field[:, :1], ROWS, -1)
    return jnp.concatenate([above, field, below], axis=1)


def chip_at(place, chips):
    far = place // (chips // 2)
    return (1 - far) * (2 * place) + far * (2 * (chips - 1 - place) + 1)


def place_of(chip, chips):
    odd = chip % 2
    return (1 - odd) * (chip // 2) + odd * (chips - 1 - chip // 2)


def meet(chips, rows, chip, row, onward, back):
    barrier = pltpu.get_barrier_semaphore()

    def greet(**where):
        pl.semaphore_signal(
            barrier, inc=1, device_id=where, device_id_type=pl.DeviceIdType.MESH
        )

    greet(chips=onward)
    greet(chips=back)

    @pl.when(row > 0)
    def _():
        greet(rows=row - 1)

    @pl.when(row < rows - 1)
    def _():
        greet(rows=row + 1)

    sides = (row + rows - 1) // rows + (2 * rows - 2 - row) // rows
    pl.semaphore_wait(barrier, 2 + sides)


def spreader(leads, chips, rows, own_ref, full_ref, z_send, z_recv, r_send, r_recv, own_sem):
    chip, row = lax.axis_index(CHIPS), lax.axis_index(ROWS)
    place = place_of(chip, chips)
    onward = chip_at((place + 1) % chips, chips)
    back = chip_at((place + chips - 1) % chips, chips)
    many = chips // 2
    lead = (slice(None),) * leads

    def own_slice():
        return own_ref.at[lead + (chip // many, chip % many)]

    def block(shard, source, piece=None):
        at = lead + (source // many, shard, source % many)
        return full_ref.at[at if piece is None else at + (piece,)]

    keep = pltpu.make_async_copy(
        own_ref, full_ref.at[lead + (slice(None), row)], own_sem
    )

    def line(side, step):
        step_way = 1 - 2 * side
        shard = row - step_way * step
        src = own_slice() if step == 0 else block(shard, chip)
        return pltpu.make_async_remote_copy(
            src_ref=src,
            dst_ref=block(shard, chip),
            send_sem=z_send.at[side, step],
            recv_sem=z_recv.at[side, step],
            device_id={ROWS: row + step_way},
            device_id_type=pl.DeviceIdType.MESH,
        )

    def landed(side, step):
        shard = row - (1 - 2 * side) * (step + 1)
        here = block(shard, chip)
        return pltpu.make_async_remote_copy(
            src_ref=here,
            dst_ref=here,
            send_sem=z_send.at[side, step],
            recv_sem=z_recv.at[side, step],
            device_id={ROWS: row},
            device_id_type=pl.DeviceIdType.MESH,
        )

    def ring(side, step, way, turn):
        turn_way = 1 - 2 * way
        shard = row - (1 - 2 * side) * (step + 1)
        source = chip_at((place - turn_way * turn + chips) % chips, chips)
        here = block(shard, source, way)
        return pltpu.make_async_remote_copy(
            src_ref=here,
            dst_ref=here,
            send_sem=r_send.at[side, step, way, turn],
            recv_sem=r_recv.at[side, step, way, turn],
            device_id={CHIPS: back if way else onward},
            device_id_type=pl.DeviceIdType.MESH,
        )

    def ring_landed(side, step, way, turn):
        turn_way = 1 - 2 * way
        shard = row - (1 - 2 * side) * (step + 1)
        source = chip_at((place - turn_way * (turn + 1) + 2 * chips) % chips, chips)
        here = block(shard, source, way)
        return pltpu.make_async_remote_copy(
            src_ref=here,
            dst_ref=here,
            send_sem=r_send.at[side, step, way, turn],
            recv_sem=r_recv.at[side, step, way, turn],
            device_id={CHIPS: back if way else onward},
            device_id_type=pl.DeviceIdType.MESH,
        )

    def sends(side, step):
        near = row - step if side == 0 else rows - 1 - row - step
        room = rows - 1 - row if side == 0 else row
        return jnp.logical_and(near >= 0, room > 0)

    def comes(side, step):
        return (row if side == 0 else rows - 1 - row) > step

    def begin():
        keep.start()
        for side in range(2):

            @pl.when(sends(side, 0))
            def _():
                line(side, 0).start()

    def advance(tick):
        if tick < rows - 1:
            for side in range(2):

                @pl.when(comes(side, tick))
                def _():
                    landed(side, tick).wait_recv()
                    if tick + 1 < rows - 1:

                        @pl.when(sends(side, tick + 1))
                        def _():
                            line(side, tick + 1).start()

                    for way in range(2):
                        ring(side, tick, way, 0).start()

        for turn in range(1, chips):
            step = tick - turn
            if 0 <= step < rows - 1:
                for side in range(2):

                    @pl.when(comes(side, step))
                    def _():
                        for way in range(2):
                            ring_landed(side, step, way, turn - 1).wait_recv()
                            if turn < chips - 1:
                                ring(side, step, way, turn).start()

    def finish():
        for side in range(2):
            for step in range(rows - 1):

                @pl.when(sends(side, step))
                def _():
                    line(side, step).wait_send()

                @pl.when(comes(side, step))
                def _():
                    for way in range(2):
                        for turn in range(chips - 1):
                            ring(side, step, way, turn).wait_send()

    return begin, advance, finish, keep


def spread_kernel(leads, chips, rows, *refs):
    chip, row = lax.axis_index(CHIPS), lax.axis_index(ROWS)
    place = place_of(chip, chips)
    onward = chip_at((place + 1) % chips, chips)
    back = chip_at((place + chips - 1) % chips, chips)
    meet(chips, rows, chip, row, onward, back)
    begin, advance, finish, keep = spreader(leads, chips, rows, *refs)
    begin()
    for tick in range(rows - 1 + chips - 1):
        advance(tick)
    finish()
    keep.wait()


def semaphores(chips, rows):
    return [
        pltpu.SemaphoreType.DMA((2, rows - 1)),
        pltpu.SemaphoreType.DMA((2, rows - 1)),
        pltpu.SemaphoreType.DMA((2, rows - 1, 2, chips - 1)),
        pltpu.SemaphoreType.DMA((2, rows - 1, 2, chips - 1)),
        pltpu.SemaphoreType.DMA,
    ]


GROUPS = 4


def drive_kernel(chips, rows, in_ref, out_ref, field_ref, driven_ref, full_out, full_in, views, *sems):
    chip, row = lax.axis_index(CHIPS), lax.axis_index(ROWS)
    place = place_of(chip, chips)
    onward = chip_at((place + 1) % chips, chips)
    back = chip_at((place + chips - 1) % chips, chips)
    meet(chips, rows, chip, row, onward, back)
    count = len(sems) // 2
    first = spreader(0, chips, rows, in_ref, full_in, *sems[:count])
    second = spreader(1, chips, rows, out_ref, full_out, *sems[count:])
    ticks, delay = rows - 1 + chips - 1, rows - 1
    total, padded, columns, channels = field_ref.shape
    band = padded - 2
    group = total // GROUPS

    def compute(index):
        at = index * group
        taps = [
            views[b, at : at + group, a : a + band].reshape(group * band * columns, channels)
            for a in range(3)
            for b in range(3)
        ]
        window = jnp.concatenate(taps, axis=1)
        for part in range(2):
            weight = full_in[part]
            weight = weight.reshape(-1, weight.shape[-1])
            states = weight.shape[0]
            driven_ref[pl.ds(index * window.shape[0], window.shape[0]), part * states : (part + 1) * states] = (
                lax.dot_general(
                    window, weight, (((1,), (1,)), ((), ())), preferred_element_type=jnp.float32
                )
            )

    first[0]()

    @pl.loop(0, total)
    def _(frame):
        whole = field_ref[frame]
        wide = whole.astype(jnp.float32)
        edge = jnp.zeros((padded, 1, channels), jnp.float32)
        before = jnp.concatenate([edge, wide[:, : columns - 1]], axis=1)
        after = jnp.concatenate([wide[:, 1:], edge], axis=1)
        views[0, frame] = before.astype(whole.dtype)
        views[1, frame] = whole
        views[2, frame] = after.astype(whole.dtype)

    for tick in range(ticks):
        first[1](tick)
        if tick == delay - 1:
            second[0]()
        if tick >= delay:
            second[1](tick - delay)
    first[3].wait()
    for index in range(GROUPS):
        compute(index)
        if ticks - delay + index < ticks:
            second[1](ticks - delay + index)
    for tick in range(ticks - delay + GROUPS, ticks):
        second[1](tick)
    first[2]()
    second[2]()
    second[3].wait()


def drive(own_in, own_out, field, chips, rows):
    many_in = own_in.shape[:1] + (rows,) + own_in.shape[1:]
    many_out = own_out.shape[:2] + (rows,) + own_out.shape[2:]
    total, padded, columns, channels = field.shape
    pixels = total * (padded - 2) * columns
    states = many_in[1] * many_in[2] * many_in[3] * many_in[4]
    vmem = pl.BlockSpec(memory_space=pltpu.VMEM)
    return pl.pallas_call(
        functools.partial(drive_kernel, chips, rows),
        out_shape=(
            jax.ShapeDtypeStruct((pixels, 2 * states), jnp.float32),
            jax.ShapeDtypeStruct(many_out, own_out.dtype),
        ),
        in_specs=[vmem, vmem, vmem],
        out_specs=(vmem, pl.BlockSpec(memory_space=pl.ANY)),
        scratch_shapes=[
            pltpu.VMEM(many_in, own_in.dtype),
            pltpu.VMEM((3,) + field.shape, field.dtype),
        ]
        + semaphores(chips, rows)
        + semaphores(chips, rows),
        compiler_params=pltpu.CompilerParams(
            collective_id=2, has_side_effects=True, vmem_limit_bytes=60 * 1024 * 1024
        ),
    )(own_in, own_out, field)


def spread(own, leads, chips, rows, number):
    shape = own.shape[: leads + 1] + (rows,) + own.shape[leads + 1 :]
    any_space = pl.BlockSpec(memory_space=pl.ANY)
    return pl.pallas_call(
        functools.partial(spread_kernel, leads, chips, rows),
        out_shape=jax.ShapeDtypeStruct(shape, own.dtype),
        in_specs=[pl.BlockSpec(memory_space=pltpu.VMEM)],
        out_specs=any_space,
        scratch_shapes=semaphores(chips, rows),
        compiler_params=pltpu.CompilerParams(collective_id=number, has_side_effects=True),
    )(own)


def conv(field, weight, form):
    return lax.conv_general_dilated(
        field, weight, (1, 1), ((0, 0), (1, 1)),
        dimension_numbers=("NHWC", form, "NHWC"),
        preferred_element_type=jnp.float32,
    )


def recur_kernel(last_only, both_ref, begin_ref, factor_ref, result_ref):
    states = factor_ref.shape[1]
    lam_re, lam_im = factor_ref[0:1, :], factor_ref[1:2, :]
    state_re, state_im = begin_ref[0, :, :states], begin_ref[0, :, states:]
    total = both_ref.shape[0]
    for t in range(total):
        state_re, state_im = (
            lam_re * state_re - lam_im * state_im + both_ref[t, 0, :, :states],
            lam_re * state_im + lam_im * state_re + both_ref[t, 0, :, states:],
        )
        if not last_only:
            result_ref[t, 0, :, :states] = state_re.astype(result_ref.dtype)
            result_ref[t, 0, :, states:] = state_im.astype(result_ref.dtype)
    if last_only:
        result_ref[0, :, :states] = state_re.astype(result_ref.dtype)
        result_ref[0, :, states:] = state_im.astype(result_ref.dtype)


def recur(both, begin, factor, last_only):
    total, band, columns, lanes = both.shape
    frames = pl.BlockSpec((total, 1, columns, lanes), lambda i: (0, i, 0, 0))
    single = pl.BlockSpec((1, columns, lanes), lambda i: (i, 0, 0))
    shape = both.shape[1:] if last_only else both.shape
    return pl.pallas_call(
        functools.partial(recur_kernel, last_only),
        out_shape=jax.ShapeDtypeStruct(shape, jnp.bfloat16),
        grid=(band,),
        in_specs=[frames, single, pl.BlockSpec(factor.shape, lambda i: (0, 0))],
        out_specs=single if last_only else frames,
    )(both, begin, factor)


def powers(log_rate, angle, exponent):
    modulus = jnp.exp(-log_rate * exponent)
    return modulus * jnp.cos(angle * exponent), modulus * jnp.sin(angle * exponent)


ORDER = (1, 0, 2)


def power(re, im, exponent):
    out_re, out_im = jnp.ones_like(re), jnp.zeros_like(im)
    while exponent:
        if exponent % 2:
            out_re, out_im = out_re * re - out_im * im, out_re * im + out_im * re
        re, im = re * re - im * im, 2.0 * (re * im)
        exponent //= 2
    return out_re, out_im


def layer_kernel(
    win, wout, frames, start, rate_in, angle_in, skip_in, out,
    rate, angle, skip, done, started, begin, views, full_in, full_out, driven, held, acc, tail, tail_half, met, joint, far_joint, given, got,
    z_send, z_recv, x_send, x_recv, y_send, y_recv,
    halo_send, halo_recv, pass_send, pass_recv, edge_send, edge_recv,
    first_send, first_recv, second_send, second_recv, swap_send, swap_recv, part_send, part_recv, local, out_sem,
):
    chip, core, row = (lax.axis_index(a) for a in (CHIPS, CORE, ROWS))
    rows = lax.axis_size(ROWS)
    other = 1 - core
    beside = chip + 1 - 2 * (chip % 2)
    across = (chip + 2) % 4
    opposite = 3 - chip
    _, many, padded, columns, channels = views.shape
    band, mine = padded - 2, many // 2
    lanes = tail.shape[-1] // 2
    depth = 3 * channels
    near = row // 2
    slots = (near, 1 - near)
    turns = (row + 1 - 2 * (row % 2), 2 - near, 3 * (1 - near))
    here = pl.multiple_of(core * mine, mine)
    there = pl.multiple_of(other * mine, mine)
    has_up, has_down = row > 0, row < rows - 1

    def remote(src, dst, send, recv, **where):
        return pltpu.make_async_remote_copy(
            src_ref=src, dst_ref=dst, send_sem=send, recv_sem=recv,
            device_id=where, device_id_type=pl.DeviceIdType.MESH,
        )

    def block(w, shard, quarter, o):
        a, pair, j = ORDER[o], shard // 2, shard % 2
        if w == 0:
            return full_in.at[pair, :, j, quarter, :, a * depth : (a + 1) * depth]
        return full_out.at[a, :, pair, :, j, quarter]

    def source(w, quarter, o):
        a = ORDER[o]
        if w == 0:
            return win.at[:, core, quarter, :, a * depth : (a + 1) * depth]
        return wout.at[a, :, :, core, quarter]

    def z_copy(w, shard, k, kind, first, to):
        quarter, o = (chip, k) if k < 3 else (opposite, 2)
        dst = block(w, shard, quarter, o)
        src = source(w, quarter, o) if first else dst
        return remote(src, dst, z_send.at[w, kind, k], z_recv.at[w, shard, k], **{ROWS: to})

    def x_copy(w, turn, i):
        quarter, o = (chip, i) if i < 3 else (across, 1)
        ref = block(w, turns[turn], quarter, o)
        return remote(ref, ref, x_send.at[w, turn, i], x_recv.at[w, turn, i], **{CHIPS: beside})

    def y_copy(w, turn, i):
        quarter, o = (chip, i) if i < 3 else (beside, 0)
        ref = block(w, turns[turn], quarter, o)
        return remote(ref, ref, y_send.at[w, turn, i], y_recv.at[w, turn, i], **{CHIPS: across})

    def x_came(w, turn, i):
        quarter, o = (beside, i) if i < 3 else (opposite, 1)
        ref = block(w, turns[turn], quarter, o)
        remote(ref, ref, x_send.at[w, turn, i], x_recv.at[w, turn, i], **{CHIPS: beside}).wait_recv()

    def y_came(w, turn, i):
        quarter, o = (across, i) if i < 3 else (opposite, 0)
        ref = block(w, turns[turn], quarter, o)
        remote(ref, ref, y_send.at[w, turn, i], y_recv.at[w, turn, i], **{CHIPS: across}).wait_recv()

    def relays(turn):
        below = turns[turn] > row
        return jnp.logical_and(below, has_up), jnp.logical_and(jnp.logical_not(below), has_down)

    inner = jnp.logical_and(has_up, has_down)
    mate_up = row % 2 == 1
    early_up = jnp.logical_and(has_up, jnp.logical_or(jnp.logical_not(inner), jnp.logical_not(mate_up)))
    early_down = jnp.logical_and(has_down, jnp.logical_or(jnp.logical_not(inner), mate_up))

    def send_own(w, ks, up=has_up, down=has_down):
        for k in ks:
            @pl.when(up)
            def _():
                z_copy(w, row, k, 3, True, row - 1).start()

            @pl.when(down)
            def _():
                z_copy(w, row, k, 4, True, row + 1).start()

    late_up = jnp.logical_and(has_up, jnp.logical_not(early_up))
    late_down = jnp.logical_and(has_down, jnp.logical_not(early_down))

    def send_early(w):
        send_own(w, range(4), early_up, early_down)

    def send_late(w, which):
        send_own(
            w, range(4), jnp.logical_and(late_up, core == which), jnp.logical_and(late_down, core == which)
        )

    def bring(w, turn, k):
        shard = turns[turn]
        z_copy(w, shard, k, turn, False, row).wait_recv()
        up, down = relays(turn)

        @pl.when(up)
        def _():
            z_copy(w, shard, k, turn, False, row - 1).start()

        @pl.when(down)
        def _():
            z_copy(w, shard, k, turn, False, row + 1).start()

    def fan(w, turn, k, x=True, y=True):
        if x:
            x_copy(w, turn, k).start()
        if y:
            y_copy(w, turn, k).start()

    def z_event(w, turn, k):
        bring(w, turn, k)
        if k < 3:
            fan(w, turn, k)

    def x_event(w, turn):
        x_came(w, turn, 0)
        y_copy(w, turn, 3).start()

    def y_event(w, turn):
        y_came(w, turn, 1)
        x_copy(w, turn, 3).start()

    def events(w, turn):
        return [
            functools.partial(z_event, w, turn, 0),
            functools.partial(z_event, w, turn, 1),
            functools.partial(x_event, w, turn),
            functools.partial(z_event, w, turn, 2),
            functools.partial(y_event, w, turn),
            functools.partial(z_event, w, turn, 3),
        ]

    def came(w, turn, o):
        if o != 0:
            x_came(w, turn, o)
        else:
            y_came(w, turn, 3)
        if o != 1:
            y_came(w, turn, o)
        else:
            x_came(w, turn, 3)

    def complete(w, rank, o):
        for turn in ((1, 2) if rank else (0,)):
            came(w, turn, o)

    def settle(w):
        for k in range(4):
            @pl.when(has_up)
            def _():
                z_copy(w, row, k, 3, True, row - 1).wait_send()

            @pl.when(has_down)
            def _():
                z_copy(w, row, k, 4, True, row + 1).wait_send()

            for turn in range(3):
                up, down = relays(turn)

                @pl.when(jnp.logical_or(up, down))
                def _():
                    z_copy(w, turns[turn], k, turn, False, row).wait_send()

        for turn in range(3):
            for i in range(4):
                x_copy(w, turn, i).wait_send()
                y_copy(w, turn, i).wait_send()

    barrier = pltpu.get_barrier_semaphore()

    def greet(**where):
        pl.semaphore_signal(barrier, inc=1, device_id=where, device_id_type=pl.DeviceIdType.MESH)

    greet(**{CORE: other})
    greet(**{CHIPS: beside})
    greet(**{CHIPS: across})

    @pl.when(has_up)
    def _():
        greet(**{ROWS: row - 1})

    @pl.when(has_down)
    def _():
        greet(**{ROWS: row + 1})

    pl.semaphore_wait(barrier, 3 + (row + rows - 1) // rows + (2 * rows - 2 - row) // rows)

    mine_in = views.at[1, pl.ds(here, mine), 1 : band + 1]
    keep = pltpu.make_async_copy(frames, mine_in, local.at[0])
    hold_in = pltpu.make_async_copy(win.at[:, core], full_in.at[near, :, row % 2], local.at[1])
    hold_out = pltpu.make_async_copy(wout.at[:, :, :, core], full_out.at[:, :, near, :, row % 2], local.at[2])
    hold_start = pltpu.make_async_copy(start, started, local.at[3])
    swap = remote(frames, mine_in, swap_send, swap_recv, **{CORE: other})
    theirs_in = views.at[1, pl.ds(there, mine), 1 : band + 1]

    def halo(side, start):
        at = views.at[1, pl.ds(here, mine), band + 1 if side == 0 else 0]
        src = frames.at[:, 0 if side == 0 else band - 1]
        return remote(src, at, halo_send.at[side], halo_recv.at[side], **{ROWS: row - 1 if side == 0 else row + 1})

    def halo_at(side, first):
        return views.at[1, pl.ds(first, mine), band + 1 if side == 0 else 0]

    def halo_came(side):
        ref = halo_at(side, here)
        remote(ref, ref, halo_send.at[side], halo_recv.at[side], **{ROWS: row}).wait_recv()

    def handed(side, first):
        ref = halo_at(side, first)
        return remote(ref, ref, pass_send.at[side], pass_recv.at[side], **{CORE: other})

    gives = (has_up, has_down)
    takes = (has_down, has_up)

    send_own(0, range(4))
    held_back = (jnp.logical_and(inner, mate_up), jnp.logical_and(inner, jnp.logical_not(mate_up)))
    for side in range(2):
        @pl.when(jnp.logical_and(gives[side], jnp.logical_not(held_back[side])))
        def _():
            halo(side, True).start()

    swap.start()
    keep.start()

    small = [
        pltpu.make_async_copy(src, dst, local.at[4 + i])
        for i, (src, dst) in enumerate(((rate_in, rate), (angle_in, angle), (skip_in, skip)))
    ]
    for copy in small:
        copy.start()
    hold_in.start()
    hold_out.start()

    @pl.when(chip == 0)
    def _():
        hold_start.start()

    blank = jnp.zeros((columns, channels), views.dtype)
    for side in range(2):
        edge = band + 1 if side == 0 else 0

        @pl.when(jnp.logical_not(takes[side]))
        def _():
            @pl.loop(0, many)
            def _(f):
                views[1, f, edge] = blank
                for slot in range(2):
                    held[slot, 1, f, edge] = blank[:, : 2 * lanes]

    place = lax.broadcasted_iota(jnp.int32, (columns, 1), 0)
    not_first, not_last = place > 0, place < columns - 1

    def sides(wide):
        before = jnp.where(not_first, pltpu.roll(wide, 1, 0), 0.0)
        after = jnp.where(not_last, pltpu.roll(wide, columns - 1, 0), 0.0)
        return before.astype(views.dtype), after.astype(views.dtype)

    def spread_views(first):
        @pl.loop(0, mine)
        def _(i):
            f = first + i

            @pl.loop(1, band + 1)
            def _(r):
                views[0, f, r], views[2, f, r] = sides(views[1, f, r].astype(jnp.float32))

    def spread_edges(first):
        @pl.loop(0, mine)
        def _(i):
            f = first + i
            for r in (0, band + 1):
                views[0, f, r], views[2, f, r] = sides(views[1, f, r].astype(jnp.float32))

    def hand_over():
        for side in range(2):
            @pl.when(takes[side])
            def _():
                halo_came(side)
                handed(side, here).start()

        spread_edges(here)

    def take_over():
        for side in range(2):
            @pl.when(takes[side])
            def _():
                handed(side, there).wait_recv()

        spread_edges(there)

    def drive(rank, o, m0, m1):
        slot, a = slots[rank], ORDER[o]

        @pl.loop(m0, m1)
        def _(m):
            at = pl.ds(m * 2, 2)
            pixels = 2 * band * columns
            window = jnp.concatenate(
                [views[b, at, a : a + band].reshape(pixels, channels) for b in range(3)], axis=1
            )
            weight = full_in[slot, :, :, :, :, a * depth : (a + 1) * depth].reshape(2 * lanes, depth)
            result = lax.dot_general(
                window, weight, (((1,), (1,)), ((), ())), preferred_element_type=jnp.float32
            ).reshape(2, band, columns, 2 * lanes)
            if o == 0:
                driven[slot, at] = result
            else:
                driven[slot, at] += result

    blocks = many // 2

    low = lax.broadcasted_iota(jnp.int32, (1, lanes), 1) < lanes // 2

    def joined(first, second):
        first = jnp.where(core == 0, first, pltpu.roll(first, lanes // 2, 1))
        second = jnp.where(core == 0, pltpu.roll(second, lanes // 2, 1), second)
        return jnp.where(low, first, second)

    def factors(rank):
        def lane_row(ref):
            first, second = (
                jnp.broadcast_to(ref[pl.ds(2 * slots[rank] + j, 1), :], (8, lanes)) for j in range(2)
            )
            return joined(first, second)[:1]

        modulus, turn = jnp.exp(-lane_row(rate)), lane_row(angle)
        return modulus * jnp.cos(turn), modulus * jnp.sin(turn)

    def prepare():
        @pl.when(chip == 0)
        def _():
            hold_start.wait()

            @pl.loop(0, band)
            def _(r):
                for pair in range(2):
                    for part in range(2):
                        at = slice(part * lanes, (part + 1) * lanes)
                        begin[pair, r, :, at] = joined(
                            started[r, :, 4 * pair + part], started[r, :, 4 * pair + 2 + part]
                        )

        @pl.when(chip > 0)
        def _():
            @pl.loop(0, band)
            def _(r):
                for pair in range(2):
                    begin[pair, r] = jnp.zeros((columns, 2 * lanes), jnp.float32)

    def ends(rank):
        slot = slots[rank]
        lam_re, lam_im = factors(rank)

        @pl.loop(0, band)
        def _(r):
            re, im = begin[slot, r, :, :lanes], begin[slot, r, :, lanes:]
            for t in range(many):
                re, im = (
                    lam_re * re - lam_im * im + driven[slot, t, r, :, :lanes],
                    lam_re * im + lam_im * re + driven[slot, t, r, :, lanes:],
                )
            tail[slot, r, :, :lanes] = re
            tail[slot, r, :, lanes:] = im
            tail_half[slot, r, :, :lanes] = re.astype(tail_half.dtype)
            tail_half[slot, r, :, lanes:] = im.astype(tail_half.dtype)

    tells, hears = chip < 3, chip != 2
    joins = chip < 2

    def first_copy(rank):
        slot = slots[rank]
        return remote(
            tail_half.at[slot], met.at[slot], first_send.at[rank], first_recv.at[rank], **{CHIPS: beside}
        )

    def second_copy(rank):
        slot = slots[rank]
        return remote(
            joint.at[slot], far_joint.at[slot], second_send.at[rank], second_recv.at[rank], **{CHIPS: across}
        )

    def tell(rank):
        @pl.when(tells)
        def _():
            first_copy(rank).start()

    def merge(rank):
        slot = slots[rank]
        lam_re, lam_im = factors(rank)
        jump_re, jump_im = power(lam_re, lam_im, many)

        def combine(r, late_re, late_im, early_re, early_im):
            return (
                late_re + jump_re * early_re - jump_im * early_im,
                late_im + jump_re * early_im + jump_im * early_re,
            )

        def split(ref, r):
            return ref[slot, r, :, :lanes].astype(jnp.float32), ref[slot, r, :, lanes:].astype(jnp.float32)

        def put(ref, r, value):
            ref[slot, r, :, :lanes] = value[0].astype(ref.dtype)
            ref[slot, r, :, lanes:] = value[1].astype(ref.dtype)

        @pl.when(hears)
        def _():
            first_copy(rank).wait_recv()

        @pl.when(chip == 0)
        def _():
            @pl.loop(0, band)
            def _(r):
                put(joint, r, combine(r, *split(met, r), *split(tail, r)))
                put(tail, r, split(begin, r))

        @pl.when(chip == 1)
        def _():
            @pl.loop(0, band)
            def _(r):
                put(joint, r, combine(r, *split(tail, r), *split(met, r)))
                put(tail, r, split(met, r))

        @pl.when(joins)
        def _():
            second_copy(rank).start()

    def carry(rank):
        slot = slots[rank]
        lam_re, lam_im = factors(rank)
        jump_re, jump_im = power(lam_re, lam_im, many)

        @pl.when(jnp.logical_not(joins))
        def _():
            second_copy(rank).wait_recv()

        @pl.when(chip == 2)
        def _():
            @pl.loop(0, band)
            def _(r):
                tail[slot, r] = far_joint[slot, r].astype(jnp.float32)

        @pl.when(chip == 3)
        def _():
            @pl.loop(0, band)
            def _(r):
                late, early = met[slot, r].astype(jnp.float32), far_joint[slot, r].astype(jnp.float32)
                re, im = early[:, :lanes], early[:, lanes:]
                tail[slot, r, :, :lanes] = late[:, :lanes] + jump_re * re - jump_im * im
                tail[slot, r, :, lanes:] = late[:, lanes:] + jump_re * im + jump_im * re

    def scan_rows(rank, start, count, stride):
        slot = slots[rank]
        lam_re, lam_im = factors(rank)

        @pl.loop(0, count)
        def _(i):
            r = start + i * stride
            re, im = tail[slot, r, :, :lanes], tail[slot, r, :, lanes:]
            for t in range(many):
                re, im = (
                    lam_re * re - lam_im * im + driven[slot, t, r, :, :lanes],
                    lam_re * im + lam_im * re + driven[slot, t, r, :, lanes:],
                )
                for part, value in enumerate((re, im)):
                    at = slice(part * lanes, (part + 1) * lanes)
                    before, after = sides(value)
                    held[slot, 0, t, 1 + r, :, at] = before
                    held[slot, 1, t, 1 + r, :, at] = value.astype(held.dtype)
                    held[slot, 2, t, 1 + r, :, at] = after

    def edge_copy(rank, side):
        slot = slots[rank]
        return remote(
            held.at[slot, 1, :, 1 if side == 0 else band],
            held.at[slot, 1, :, band + 1 if side == 0 else 0],
            edge_send.at[rank, side],
            edge_recv.at[slot, side],
            **{ROWS: row - 1 if side == 0 else row + 1},
        )

    def scan(rank):
        scan_rows(rank, 0, 2, band - 1)
        scan_rows(rank, 1, (band - 2) // 2, 1)
        for side in range(2):
            @pl.when(gives[side])
            def _():
                edge_copy(rank, side).start()
        scan_rows(rank, 1 + (band - 2) // 2, band - 2 - (band - 2) // 2, 1)

    def edges_came(rank):
        slot = slots[rank]
        for side in range(2):
            at = band + 1 if side == 0 else 0
            ref = held.at[slot, 1, :, at]

            @pl.when(takes[side])
            def _():
                remote(
                    ref, ref, edge_send.at[rank, side], edge_recv.at[slot, side], **{ROWS: row}
                ).wait_recv()

            @pl.loop(0, many)
            def _(f):
                held[slot, 0, f, at], held[slot, 2, f, at] = sides(held[slot, 1, f, at].astype(jnp.float32))

    def mix_block(rank, rights, first, fresh):
        slot = slots[rank]
        pixels = 2 * band * columns
        window = jnp.concatenate(
            [
                held[slot, b, pl.ds(first, 2), a : a + band].reshape(pixels, 2 * lanes)
                for a in rights
                for b in range(3)
            ],
            axis=1,
        )
        weight = jnp.concatenate([full_out[a, :, slot].reshape(6 * lanes, channels) for a in rights], axis=0)
        result = jnp.dot(window, weight, preferred_element_type=jnp.float32)
        result = result.reshape(2, band, columns, channels)
        if fresh:
            return result
        return acc[pl.ds(first, 2)] + result

    def mix(rank, rights, fresh, m0=0, m1=None):
        @pl.loop(m0, blocks if m1 is None else m1)
        def _(m):
            acc[pl.ds(m * 2, 2)] = mix_block(rank, rights, m * 2, fresh)

    def part_copy(m):
        at = pl.ds(m * 2, 2)
        return remote(
            given.at[at], got.at[at], part_send.at[m], part_recv.at[m], **{CORE: other}
        )

    def out_copy(f):
        return pltpu.make_async_copy(done.at[f], out.at[f], out_sem.at[f])

    def mix_last(rank, rights):
        for m in range(blocks // 2):
            given[m * 2 : m * 2 + 2] = mix_block(rank, rights, there + m * 2, False).astype(given.dtype)
            part_copy(m).start()
        for m in range(blocks // 2):
            acc[pl.ds(here + m * 2, 2)] = mix_block(rank, rights, here + m * 2, False)
        for m in range(blocks // 2):
            part_copy(m).wait_recv()

            @pl.loop(0, 2)
            def _(i):
                f = m * 2 + i

                @pl.loop(0, band)
                def _(r):
                    value = acc[here + f, r] + got[f, r].astype(jnp.float32)
                    value = value + skip[...] * views[1, here + f, 1 + r].astype(jnp.float32)
                    done[f, r] = (0.5 * value * (1.0 + lax.erf(value * 0.7071067811865476))).astype(done.dtype)

                out_copy(f).start()

    steps = iter(events(0, 0))
    next(steps)()
    next(steps)()

    @pl.when(inner)
    def _():
        bring(0, 1, 0)
        bring(0, 1, 1)
        for side in range(2):
            @pl.when(held_back[side])
            def _():
                halo(side, True).start()

    keep.wait()
    spread_views(here)
    next(steps)()
    next(steps)()
    prepare()
    next(steps)()
    next(steps)()
    remote(theirs_in, theirs_in, swap_send, swap_recv, **{CORE: other}).wait_recv()
    spread_views(there)
    hold_in.wait()
    hold_out.wait()
    for copy in small:
        copy.wait()
    half = blocks // 2

    @pl.when(inner)
    def _():
        fan(0, 1, 0)
        bring(0, 1, 2)
        bring(0, 1, 3)
        fan(0, 1, 1)
        complete(0, 0, 0)
        drive(0, 0, 0, half)
        fan(0, 1, 2)
        drive(0, 0, half, blocks)
        hand_over()
        z_event(0, 2, 0)
        x_event(0, 1)
        take_over()
        complete(0, 0, 1)
        drive(0, 1, 0, half)
        z_event(0, 2, 1)
        y_event(0, 1)
        drive(0, 1, half, blocks)
        z_event(0, 2, 2)
        z_event(0, 2, 3)
        send_early(1)
        send_late(1, 0)
        complete(0, 0, 2)
        drive(0, 2, 0, blocks)
        ends(0)
        x_event(0, 2)
        y_event(0, 2)
        tell(0)
        complete(0, 1, 0)
        drive(1, 0, 0, blocks)
        send_late(1, 1)
        bring(1, 0, 2)
        bring(1, 0, 3)
        bring(1, 0, 0)
        bring(1, 0, 1)
        complete(0, 1, 1)
        fan(1, 0, 0)
        drive(1, 1, 0, blocks)
        merge(0)
        complete(0, 1, 2)
        drive(1, 2, 0, blocks)
        ends(1)
        tell(1)
        bring(1, 1, 0)
        bring(1, 1, 1)
        bring(1, 1, 2)
        bring(1, 1, 3)
        fan(1, 0, 1)
        carry(0)
        scan(0)
        bring(1, 2, 2)
        bring(1, 2, 3)
        merge(1)
        fan(1, 0, 2)
        x_event(1, 0)
        fan(1, 1, 0)
        y_event(1, 0)
        fan(1, 1, 1)
        bring(1, 2, 0)
        bring(1, 2, 1)
        fan(1, 1, 2)
        carry(1)
        scan(1)
        complete(1, 0, 0)
        mix(0, (1,), True)
        x_event(1, 1)
        fan(1, 2, 2)
        edges_came(0)
        complete(1, 0, 1)
        mix(0, (0,), False)
        y_event(1, 1)
        fan(1, 2, 0)
        fan(1, 2, 1)
        complete(1, 0, 2)
        mix(0, (2,), False)
        edges_came(1)
        complete(1, 1, 2)
        mix(1, (2,), False, 0, half)
        x_event(1, 2)
        mix(1, (2,), False, half)
        y_event(1, 2)
        complete(1, 1, 0)
        mix(1, (1,), False)
        complete(1, 1, 1)

    @pl.when(jnp.logical_not(inner))
    def _():
        z_event(0, 1, 0)
        complete(0, 0, 0)
        drive(0, 0, 0, half)
        z_event(0, 1, 1)
        drive(0, 0, half, blocks)
        x_event(0, 1)
        hand_over()
        take_over()
        complete(0, 0, 1)
        drive(0, 1, 0, half)
        z_event(0, 1, 2)
        send_early(1)
        drive(0, 1, half, blocks)
        y_event(0, 1)
        z_event(0, 1, 3)
        complete(0, 0, 2)
        drive(0, 2, 0, half)
        z_event(0, 2, 0)
        drive(0, 2, half, blocks)
        z_event(0, 2, 1)
        ends(0)
        x_event(0, 2)
        z_event(0, 2, 2)
        y_event(0, 2)
        tell(0)
        complete(0, 1, 0)
        drive(1, 0, 0, blocks)
        z_event(0, 2, 3)
        bring(1, 0, 0)
        fan(1, 0, 0)
        complete(0, 1, 1)
        drive(1, 1, 0, blocks)
        merge(0)
        bring(1, 0, 1)
        fan(1, 0, 1)
        complete(0, 1, 2)
        drive(1, 2, 0, blocks)
        ends(1)
        tell(1)
        carry(0)
        scan(0)
        bring(1, 0, 2)
        fan(1, 0, 2, x=False)
        merge(1)
        fan(1, 0, 2, y=False)
        x_event(1, 0)
        bring(1, 0, 3)
        z_event(1, 1, 0)
        y_event(1, 0)
        z_event(1, 1, 1)
        carry(1)
        scan(1)
        z_event(1, 1, 2)
        complete(1, 0, 0)
        mix(0, (1,), True, 0, half)
        x_event(1, 1)
        mix(0, (1,), True, half)
        z_event(1, 1, 3)
        z_event(1, 2, 2)
        edges_came(0)
        complete(1, 0, 1)
        mix(0, (0,), False, 0, half)
        z_event(1, 2, 3)
        y_event(1, 1)
        mix(0, (0,), False, half)
        z_event(1, 2, 0)
        complete(1, 0, 2)
        mix(0, (2,), False, 0, half)
        z_event(1, 2, 1)
        mix(0, (2,), False, half)
        x_event(1, 2)
        edges_came(1)
        complete(1, 1, 2)
        mix(1, (2,), False, 0, half)
        y_event(1, 2)
        mix(1, (2,), False, half)
        complete(1, 1, 0)
        mix(1, (1,), False)
        complete(1, 1, 1)

    mix_last(1, (0,))
    settle(0)
    settle(1)
    swap.wait_send()
    for side in range(2):
        @pl.when(gives[side])
        def _():
            halo(side, False).wait_send()
            for rank in range(2):
                edge_copy(rank, side).wait_send()

        @pl.when(takes[side])
        def _():
            handed(side, here).wait_send()

    for rank in range(2):
        @pl.when(tells)
        def _():
            first_copy(rank).wait_send()

        @pl.when(joins)
        def _():
            second_copy(rank).wait_send()

    for m in range(blocks // 2):
        part_copy(m).wait_send()

    for f in range(mine):
        out_copy(f).wait()


def layer(weight_in, weight_out, frames_in, start, log_decay, rotation, skip_gain):
    count, band, columns, channels = frames_in.shape
    lanes = weight_in.shape[1]
    quarter = lanes // 8
    many = 2 * count
    anywhere = pl.BlockSpec(memory_space=pl.ANY)
    dma = pltpu.SemaphoreType.DMA
    half = frames_in.dtype
    full = jnp.float32
    return pl.pallas_call(
        layer_kernel,
        out_shape=jax.ShapeDtypeStruct(frames_in.shape, half),
        in_specs=[anywhere] * 7,
        out_specs=anywhere,
        scratch_shapes=[
            pltpu.VMEM((log_decay.size // lanes, lanes), full),
            pltpu.VMEM((log_decay.size // lanes, lanes), full),
            pltpu.VMEM((1, channels), full),
            pltpu.VMEM(frames_in.shape, half),
            pltpu.VMEM(start.shape, full),
            pltpu.VMEM((2, band, columns, 2 * lanes), full),
            pltpu.VMEM((3, many, band + 2, columns, channels), half),
            pltpu.VMEM((2, 2, 2, 4, quarter, 9 * channels), half),
            pltpu.VMEM((3, 3, 2, 2, 2, 4, quarter, channels), half),
            pltpu.VMEM((2, many, band, columns, 2 * lanes), full),
            pltpu.VMEM((2, 3, many, band + 2, columns, 2 * lanes), half),
            pltpu.VMEM((many, band, columns, channels), full),
            pltpu.VMEM((2, band, columns, 2 * lanes), full),
            pltpu.VMEM((2, band, columns, 2 * lanes), half),
            pltpu.VMEM((2, band, columns, 2 * lanes), half),
            pltpu.VMEM((2, band, columns, 2 * lanes), half),
            pltpu.VMEM((2, band, columns, 2 * lanes), half),
            pltpu.VMEM((count, band, columns, channels), half),
            pltpu.VMEM((count, band, columns, channels), half),
            dma((2, 5, 4)), dma((2, 4, 4)), dma((2, 3, 4)), dma((2, 3, 4)), dma((2, 3, 4)), dma((2, 3, 4)),
            dma((2,)), dma((2,)), dma((2,)), dma((2,)), dma((2, 2)), dma((2, 2)),
            dma((2,)), dma((2,)), dma((2,)), dma((2,)), dma, dma,
            dma((many // 4,)), dma((many // 4,)), dma((7,)), dma((count,)),
        ],
        compiler_params=pltpu.CompilerParams(
            collective_id=3, has_side_effects=True, vmem_limit_bytes=63 * 1024 * 1024
        ),
    )(
        weight_in.reshape(2, 2, 4, quarter, 9 * channels),
        weight_out.reshape(3, 3, 2, 2, 4, quarter, channels),
        frames_in,
        start,
        log_decay.reshape(-1, lanes),
        rotation.reshape(-1, lanes),
        skip_gain.reshape(1, channels),
    )


def fused(frames_in, weight_in, weight_out, log_decay, rotation, start_state, skip_gain):
    lanes = weight_in.shape[1]
    band, columns = start_state.shape[:2]
    start = start_state.reshape(band, columns, 2, -1, lanes).swapaxes(2, 3).reshape(band, columns, -1, lanes)
    return layer(weight_in, weight_out, frames_in, start, log_decay, rotation, skip_gain)


def fits(frames_in, weight_in):
    count, band, columns, channels = frames_in.shape
    chips, cores, rows = (lax.axis_size(a) for a in (CHIPS, CORE, ROWS))
    return (
        (chips, rows) == (4, 2 * cores)
        and weight_in.shape[1] % 128 == 0
        and channels % 128 == 0
        and columns % 16 == 0
        and band >= 4
        and count % 4 == 0
    )


def on_device(frames_in, weight_in, weight_out, log_decay, rotation, start_state, skip_gain):
    if fits(frames_in, weight_in):
        return fused(frames_in, weight_in, weight_out, log_decay, rotation, start_state, skip_gain)
    frame_count, band_rows, columns, channels = frames_in.shape
    shard = weight_in.shape[1]
    chips, cores, rows = (lax.axis_size(a) for a in (CHIPS, CORE, ROWS))
    core, chip = lax.axis_index(CORE), lax.axis_index(CHIPS)
    half = shard // cores
    many = chips // 2
    piece = half // (2 * many)

    def own(vector, axis):
        picks = [
            jnp.concatenate(
                [
                    lax.slice_in_dim(vector, r * shard + c * half, r * shard + (c + 1) * half, axis=axis)
                    for r in range(rows)
                ],
                axis=axis,
            )
            for c in range(cores)
        ]
        return jnp.where(core == 0, picks[0], picks[1])

    states = rows * half
    slice_in = lax.dynamic_slice_in_dim(weight_in, core * half, half, 1)
    slice_out = lax.dynamic_slice_in_dim(weight_out, core * half, half, 2)
    own_in = slice_in.reshape(2, many, 2, piece, 9 * channels)
    own_out = slice_out.reshape(9, 2, many, 2, piece, channels)

    mine = with_halo(frames_in)
    theirs = swapped(mine)
    first = jnp.where(core == 0, mine, theirs)
    second = jnp.where(core == 0, theirs, mine)
    field = jnp.concatenate([first, second], axis=0)
    total = field.shape[0]

    if piece % 16 == 0 and total % GROUPS == 0:
        both, out_full = drive(own_in, own_out, field, chips, rows)
        both = both.reshape(total, band_rows, columns, 2 * states)
    else:
        in_full = spread(own_in, 0, chips, rows, 0).reshape(2, states, 3, 3, channels)
        out_full = spread(own_out, 1, chips, rows, 1)
        both = jnp.concatenate(
            [conv(field, in_full[part], "OHWI") for part in range(2)], axis=-1
        )

    log_rate, angle = own(log_decay, 0), own(rotation, 0)
    start = own(start_state, 3)
    lam_re, lam_im = powers(log_rate, angle, jnp.float32(1.0))
    begin = jnp.concatenate([start[:, :, 0], start[:, :, 1]], axis=-1)
    begin = jnp.where(chip == 0, begin, jnp.float32(0.0))
    factor = jnp.stack([lam_re, lam_im])
    tail = recur(both, begin, factor, True)
    carry_re = carry_im = jnp.float32(0.0)
    for step in range(1, chips):
        far = shifted(tail, CHIPS, step).astype(jnp.float32)
        jump_re, jump_im = powers(log_rate, angle, jnp.float32(total * (step - 1)))
        carry_re = carry_re + jump_re * far[..., :states] - jump_im * far[..., states:]
        carry_im = carry_im + jump_re * far[..., states:] + jump_im * far[..., :states]
    begin = begin + jnp.concatenate([carry_re, carry_im], axis=-1)
    held = with_halo(recur(both, begin, factor, False))

    out_weight = out_full.reshape(3, 3, 2 * states, channels)
    held_theirs = lax.dynamic_slice_in_dim(held, (1 - core) * frame_count, frame_count, 0)
    held_mine = lax.dynamic_slice_in_dim(held, core * frame_count, frame_count, 0)
    sent = conv(held_theirs, out_weight, "HWIO").astype(jnp.bfloat16)
    got = swapped(sent).astype(jnp.float32)
    mixing = conv(held_mine, out_weight, "HWIO") + got
    pre_act = mixing + skip_gain * frames_in.astype(jnp.float32)
    return jax.nn.gelu(pre_act, approximate=False).astype(jnp.bfloat16)


def solution(mesh):
    count, rows = mesh.devices.shape
    fine = Mesh(mesh.devices.reshape(count // 2, 2, rows), (CHIPS, CORE, ROWS))
    frames = P((CHIPS, CORE), ROWS, None, None)
    return jax.shard_map(
        on_device,
        mesh=fine,
        in_specs=(
            frames,
            P(None, ROWS, None),
            P(None, None, ROWS, None),
            P(),
            P(),
            P(ROWS, None, None, None),
            P(),
        ),
        out_specs=frames,
        check_vma=False,
    )
```

```python
import functools
import jax
import jax.numpy as jnp
from jax import lax
from jax.experimental import pallas as pl
from jax.experimental.pallas import tpu as pltpu
from jax.sharding import Mesh, PartitionSpec as P

CHIPS, CORE, ROWS = "chips", "core", "rows"


def shifted(value, axis, step):
    count = lax.axis_size(axis)
    pairs = [(i, i + step) for i in range(count) if 0 <= i + step < count]
    return lax.ppermute(value, axis, pairs)


def swapped(value):
    return lax.ppermute(value, CORE, [(0, 1), (1, 0)])


def with_halo(field):
    above = shifted(field[:, -1:], ROWS, 1)
    below = shifted(field[:, :1], ROWS, -1)
    return jnp.concatenate([above, field, below], axis=1)


def chip_at(place, chips):
    far = place // (chips // 2)
    return (1 - far) * (2 * place) + far * (2 * (chips - 1 - place) + 1)


def place_of(chip, chips):
    odd = chip % 2
    return (1 - odd) * (chip // 2) + odd * (chips - 1 - chip // 2)


def meet(chips, rows, chip, row, onward, back):
    barrier = pltpu.get_barrier_semaphore()

    def greet(**where):
        pl.semaphore_signal(
            barrier, inc=1, device_id=where, device_id_type=pl.DeviceIdType.MESH
        )

    greet(chips=onward)
    greet(chips=back)

    @pl.when(row > 0)
    def _():
        greet(rows=row - 1)

    @pl.when(row < rows - 1)
    def _():
        greet(rows=row + 1)

    sides = (row + rows - 1) // rows + (2 * rows - 2 - row) // rows
    pl.semaphore_wait(barrier, 2 + sides)


def spreader(leads, chips, rows, own_ref, full_ref, z_send, z_recv, r_send, r_recv, own_sem):
    chip, row = lax.axis_index(CHIPS), lax.axis_index(ROWS)
    place = place_of(chip, chips)
    onward = chip_at((place + 1) % chips, chips)
    back = chip_at((place + chips - 1) % chips, chips)
    many = chips // 2
    lead = (slice(None),) * leads

    def own_slice():
        return own_ref.at[lead + (chip // many, chip % many)]

    def block(shard, source, piece=None):
        at = lead + (source // many, shard, source % many)
        return full_ref.at[at if piece is None else at + (piece,)]

    keep = pltpu.make_async_copy(
        own_ref, full_ref.at[lead + (slice(None), row)], own_sem
    )

    def line(side, step):
        step_way = 1 - 2 * side
        shard = row - step_way * step
        src = own_slice() if step == 0 else block(shard, chip)
        return pltpu.make_async_remote_copy(
            src_ref=src,
            dst_ref=block(shard, chip),
            send_sem=z_send.at[side, step],
            recv_sem=z_recv.at[side, step],
            device_id={ROWS: row + step_way},
            device_id_type=pl.DeviceIdType.MESH,
        )

    def landed(side, step):
        shard = row - (1 - 2 * side) * (step + 1)
        here = block(shard, chip)
        return pltpu.make_async_remote_copy(
            src_ref=here,
            dst_ref=here,
            send_sem=z_send.at[side, step],
            recv_sem=z_recv.at[side, step],
            device_id={ROWS: row},
            device_id_type=pl.DeviceIdType.MESH,
        )

    def ring(side, step, way, turn):
        turn_way = 1 - 2 * way
        shard = row - (1 - 2 * side) * (step + 1)
        source = chip_at((place - turn_way * turn + chips) % chips, chips)
        here = block(shard, source, way)
        return pltpu.make_async_remote_copy(
            src_ref=here,
            dst_ref=here,
            send_sem=r_send.at[side, step, way, turn],
            recv_sem=r_recv.at[side, step, way, turn],
            device_id={CHIPS: back if way else onward},
            device_id_type=pl.DeviceIdType.MESH,
        )

    def ring_landed(side, step, way, turn):
        turn_way = 1 - 2 * way
        shard = row - (1 - 2 * side) * (step + 1)
        source = chip_at((place - turn_way * (turn + 1) + 2 * chips) % chips, chips)
        here = block(shard, source, way)
        return pltpu.make_async_remote_copy(
            src_ref=here,
            dst_ref=here,
            send_sem=r_send.at[side, step, way, turn],
            recv_sem=r_recv.at[side, step, way, turn],
            device_id={CHIPS: back if way else onward},
            device_id_type=pl.DeviceIdType.MESH,
        )

    def sends(side, step):
        near = row - step if side == 0 else rows - 1 - row - step
        room = rows - 1 - row if side == 0 else row
        return jnp.logical_and(near >= 0, room > 0)

    def comes(side, step):
        return (row if side == 0 else rows - 1 - row) > step

    def begin():
        keep.start()
        for side in range(2):

            @pl.when(sends(side, 0))
            def _():
                line(side, 0).start()

    def advance(tick):
        if tick < rows - 1:
            for side in range(2):

                @pl.when(comes(side, tick))
                def _():
                    landed(side, tick).wait_recv()
                    if tick + 1 < rows - 1:

                        @pl.when(sends(side, tick + 1))
                        def _():
                            line(side, tick + 1).start()

                    for way in range(2):
                        ring(side, tick, way, 0).start()

        for turn in range(1, chips):
            step = tick - turn
            if 0 <= step < rows - 1:
                for side in range(2):

                    @pl.when(comes(side, step))
                    def _():
                        for way in range(2):
                            ring_landed(side, step, way, turn - 1).wait_recv()
                            if turn < chips - 1:
                                ring(side, step, way, turn).start()

    def finish():
        for side in range(2):
            for step in range(rows - 1):

                @pl.when(sends(side, step))
                def _():
                    line(side, step).wait_send()

                @pl.when(comes(side, step))
                def _():
                    for way in range(2):
                        for turn in range(chips - 1):
                            ring(side, step, way, turn).wait_send()

    return begin, advance, finish, keep


def spread_kernel(leads, chips, rows, *refs):
    chip, row = lax.axis_index(CHIPS), lax.axis_index(ROWS)
    place = place_of(chip, chips)
    onward = chip_at((place + 1) % chips, chips)
    back = chip_at((place + chips - 1) % chips, chips)
    meet(chips, rows, chip, row, onward, back)
    begin, advance, finish, keep = spreader(leads, chips, rows, *refs)
    begin()
    for tick in range(rows - 1 + chips - 1):
        advance(tick)
    finish()
    keep.wait()


def semaphores(chips, rows):
    return [
        pltpu.SemaphoreType.DMA((2, rows - 1)),
        pltpu.SemaphoreType.DMA((2, rows - 1)),
        pltpu.SemaphoreType.DMA((2, rows - 1, 2, chips - 1)),
        pltpu.SemaphoreType.DMA((2, rows - 1, 2, chips - 1)),
        pltpu.SemaphoreType.DMA,
    ]


GROUPS = 4


def drive_kernel(chips, rows, in_ref, out_ref, field_ref, driven_ref, full_out, full_in, views, *sems):
    chip, row = lax.axis_index(CHIPS), lax.axis_index(ROWS)
    place = place_of(chip, chips)
    onward = chip_at((place + 1) % chips, chips)
    back = chip_at((place + chips - 1) % chips, chips)
    meet(chips, rows, chip, row, onward, back)
    count = len(sems) // 2
    first = spreader(0, chips, rows, in_ref, full_in, *sems[:count])
    second = spreader(1, chips, rows, out_ref, full_out, *sems[count:])
    ticks, delay = rows - 1 + chips - 1, rows - 1
    total, padded, columns, channels = field_ref.shape
    band = padded - 2
    group = total // GROUPS

    def compute(index):
        at = index * group
        taps = [
            views[b, at : at + group, a : a + band].reshape(group * band * columns, channels)
            for a in range(3)
            for b in range(3)
        ]
        window = jnp.concatenate(taps, axis=1)
        for part in range(2):
            weight = full_in[part]
            weight = weight.reshape(-1, weight.shape[-1])
            states = weight.shape[0]
            driven_ref[pl.ds(index * window.shape[0], window.shape[0]), part * states : (part + 1) * states] = (
                lax.dot_general(
                    window, weight, (((1,), (1,)), ((), ())), preferred_element_type=jnp.float32
                )
            )

    first[0]()

    @pl.loop(0, total)
    def _(frame):
        whole = field_ref[frame]
        wide = whole.astype(jnp.float32)
        edge = jnp.zeros((padded, 1, channels), jnp.float32)
        before = jnp.concatenate([edge, wide[:, : columns - 1]], axis=1)
        after = jnp.concatenate([wide[:, 1:], edge], axis=1)
        views[0, frame] = before.astype(whole.dtype)
        views[1, frame] = whole
        views[2, frame] = after.astype(whole.dtype)

    for tick in range(ticks):
        first[1](tick)
        if tick == delay - 1:
            second[0]()
        if tick >= delay:
            second[1](tick - delay)
    first[3].wait()
    for index in range(GROUPS):
        compute(index)
        if ticks - delay + index < ticks:
            second[1](ticks - delay + index)
    for tick in range(ticks - delay + GROUPS, ticks):
        second[1](tick)
    first[2]()
    second[2]()
    second[3].wait()


def drive(own_in, own_out, field, chips, rows):
    many_in = own_in.shape[:1] + (rows,) + own_in.shape[1:]
    many_out = own_out.shape[:2] + (rows,) + own_out.shape[2:]
    total, padded, columns, channels = field.shape
    pixels = total * (padded - 2) * columns
    states = many_in[1] * many_in[2] * many_in[3] * many_in[4]
    vmem = pl.BlockSpec(memory_space=pltpu.VMEM)
    return pl.pallas_call(
        functools.partial(drive_kernel, chips, rows),
        out_shape=(
            jax.ShapeDtypeStruct((pixels, 2 * states), jnp.float32),
            jax.ShapeDtypeStruct(many_out, own_out.dtype),
        ),
        in_specs=[vmem, vmem, vmem],
        out_specs=(vmem, pl.BlockSpec(memory_space=pl.ANY)),
        scratch_shapes=[
            pltpu.VMEM(many_in, own_in.dtype),
            pltpu.VMEM((3,) + field.shape, field.dtype),
        ]
        + semaphores(chips, rows)
        + semaphores(chips, rows),
        compiler_params=pltpu.CompilerParams(
            collective_id=2, has_side_effects=True, vmem_limit_bytes=60 * 1024 * 1024
        ),
    )(own_in, own_out, field)


def spread(own, leads, chips, rows, number):
    shape = own.shape[: leads + 1] + (rows,) + own.shape[leads + 1 :]
    any_space = pl.BlockSpec(memory_space=pl.ANY)
    return pl.pallas_call(
        functools.partial(spread_kernel, leads, chips, rows),
        out_shape=jax.ShapeDtypeStruct(shape, own.dtype),
        in_specs=[pl.BlockSpec(memory_space=pltpu.VMEM)],
        out_specs=any_space,
        scratch_shapes=semaphores(chips, rows),
        compiler_params=pltpu.CompilerParams(collective_id=number, has_side_effects=True),
    )(own)


def conv(field, weight, form):
    return lax.conv_general_dilated(
        field, weight, (1, 1), ((0, 0), (1, 1)),
        dimension_numbers=("NHWC", form, "NHWC"),
        preferred_element_type=jnp.float32,
    )


def recur_kernel(last_only, both_ref, begin_ref, factor_ref, result_ref):
    states = factor_ref.shape[1]
    lam_re, lam_im = factor_ref[0:1, :], factor_ref[1:2, :]
    state_re, state_im = begin_ref[0, :, :states], begin_ref[0, :, states:]
    total = both_ref.shape[0]
    for t in range(total):
        state_re, state_im = (
            lam_re * state_re - lam_im * state_im + both_ref[t, 0, :, :states],
            lam_re * state_im + lam_im * state_re + both_ref[t, 0, :, states:],
        )
        if not last_only:
            result_ref[t, 0, :, :states] = state_re.astype(result_ref.dtype)
            result_ref[t, 0, :, states:] = state_im.astype(result_ref.dtype)
    if last_only:
        result_ref[0, :, :states] = state_re.astype(result_ref.dtype)
        result_ref[0, :, states:] = state_im.astype(result_ref.dtype)


def recur(both, begin, factor, last_only):
    total, band, columns, lanes = both.shape
    frames = pl.BlockSpec((total, 1, columns, lanes), lambda i: (0, i, 0, 0))
    single = pl.BlockSpec((1, columns, lanes), lambda i: (i, 0, 0))
    shape = both.shape[1:] if last_only else both.shape
    return pl.pallas_call(
        functools.partial(recur_kernel, last_only),
        out_shape=jax.ShapeDtypeStruct(shape, jnp.bfloat16),
        grid=(band,),
        in_specs=[frames, single, pl.BlockSpec(factor.shape, lambda i: (0, 0))],
        out_specs=single if last_only else frames,
    )(both, begin, factor)


def powers(log_rate, angle, exponent):
    modulus = jnp.exp(-log_rate * exponent)
    return modulus * jnp.cos(angle * exponent), modulus * jnp.sin(angle * exponent)


ORDER = (1, 0, 2)


def power(re, im, exponent):
    out_re, out_im = jnp.ones_like(re), jnp.zeros_like(im)
    while exponent:
        if exponent % 2:
            out_re, out_im = out_re * re - out_im * im, out_re * im + out_im * re
        re, im = re * re - im * im, 2.0 * (re * im)
        exponent //= 2
    return out_re, out_im


def layer_kernel(
    win, wout, frames, start, rate_in, angle_in, skip_in, out,
    rate, angle, skip, done, started, begin, views, full_in, full_out, driven, held, acc, tail, tail_half, met, joint, far_joint, given, got,
    z_send, z_recv, x_send, x_recv, y_send, y_recv,
    halo_send, halo_recv, pass_send, pass_recv, edge_send, edge_recv,
    first_send, first_recv, second_send, second_recv, swap_send, swap_recv, part_send, part_recv, local, out_sem,
):
    chip, core, row = (lax.axis_index(a) for a in (CHIPS, CORE, ROWS))
    rows = lax.axis_size(ROWS)
    other = 1 - core
    beside = chip + 1 - 2 * (chip % 2)
    across = (chip + 2) % 4
    opposite = 3 - chip
    _, many, padded, columns, channels = views.shape
    band, mine = padded - 2, many // 2
    lanes = tail.shape[-1] // 2
    depth = 3 * channels
    near = row // 2
    slots = (near, 1 - near)
    turns = (row + 1 - 2 * (row % 2), 2 - near, 3 * (1 - near))
    here = pl.multiple_of(core * mine, mine)
    there = pl.multiple_of(other * mine, mine)
    has_up, has_down = row > 0, row < rows - 1

    def remote(src, dst, send, recv, **where):
        return pltpu.make_async_remote_copy(
            src_ref=src, dst_ref=dst, send_sem=send, recv_sem=recv,
            device_id=where, device_id_type=pl.DeviceIdType.MESH,
        )

    def block(w, shard, quarter, o):
        a, pair, j = ORDER[o], shard // 2, shard % 2
        if w == 0:
            return full_in.at[pair, :, j, quarter, :, a * depth : (a + 1) * depth]
        return full_out.at[a, :, pair, :, j, quarter]

    def source(w, quarter, o):
        a = ORDER[o]
        if w == 0:
            return win.at[:, core, quarter, :, a * depth : (a + 1) * depth]
        return wout.at[a, :, :, core, quarter]

    def z_copy(w, shard, k, kind, first, to):
        quarter, o = (chip, k) if k < 3 else (opposite, 2)
        dst = block(w, shard, quarter, o)
        src = source(w, quarter, o) if first else dst
        return remote(src, dst, z_send.at[w, kind, k], z_recv.at[w, shard, k], **{ROWS: to})

    def x_copy(w, turn, i):
        quarter, o = (chip, i) if i < 3 else (across, 1)
        ref = block(w, turns[turn], quarter, o)
        return remote(ref, ref, x_send.at[w, turn, i], x_recv.at[w, turn, i], **{CHIPS: beside})

    def y_copy(w, turn, i):
        quarter, o = (chip, i) if i < 3 else (beside, 0)
        ref = block(w, turns[turn], quarter, o)
        return remote(ref, ref, y_send.at[w, turn, i], y_recv.at[w, turn, i], **{CHIPS: across})

    def x_came(w, turn, i):
        quarter, o = (beside, i) if i < 3 else (opposite, 1)
        ref = block(w, turns[turn], quarter, o)
        remote(ref, ref, x_send.at[w, turn, i], x_recv.at[w, turn, i], **{CHIPS: beside}).wait_recv()

    def y_came(w, turn, i):
        quarter, o = (across, i) if i < 3 else (opposite, 0)
        ref = block(w, turns[turn], quarter, o)
        remote(ref, ref, y_send.at[w, turn, i], y_recv.at[w, turn, i], **{CHIPS: across}).wait_recv()

    def relays(turn):
        below = turns[turn] > row
        return jnp.logical_and(below, has_up), jnp.logical_and(jnp.logical_not(below), has_down)

    inner = jnp.logical_and(has_up, has_down)
    mate_up = row % 2 == 1
    early_up = jnp.logical_and(has_up, jnp.logical_or(jnp.logical_not(inner), jnp.logical_not(mate_up)))
    early_down = jnp.logical_and(has_down, jnp.logical_or(jnp.logical_not(inner), mate_up))

    def send_own(w, ks, up=has_up, down=has_down):
        for k in ks:
            @pl.when(up)
            def _():
                z_copy(w, row, k, 3, True, row - 1).start()

            @pl.when(down)
            def _():
                z_copy(w, row, k, 4, True, row + 1).start()

    late_up = jnp.logical_and(has_up, jnp.logical_not(early_up))
    late_down = jnp.logical_and(has_down, jnp.logical_not(early_down))

    def send_early(w):
        send_own(w, range(4), early_up, early_down)

    def send_late(w, which):
        send_own(
            w, range(4), jnp.logical_and(late_up, core == which), jnp.logical_and(late_down, core == which)
        )

    def bring(w, turn, k):
        shard = turns[turn]
        z_copy(w, shard, k, turn, False, row).wait_recv()
        up, down = relays(turn)

        @pl.when(up)
        def _():
            z_copy(w, shard, k, turn, False, row - 1).start()

        @pl.when(down)
        def _():
            z_copy(w, shard, k, turn, False, row + 1).start()

    def fan(w, turn, k, x=True, y=True):
        if x:
            x_copy(w, turn, k).start()
        if y:
            y_copy(w, turn, k).start()

    def z_event(w, turn, k):
        bring(w, turn, k)
        if k < 3:
            fan(w, turn, k)

    def x_event(w, turn):
        x_came(w, turn, 0)
        y_copy(w, turn, 3).start()

    def y_event(w, turn):
        y_came(w, turn, 1)
        x_copy(w, turn, 3).start()

    def events(w, turn):
        return [
            functools.partial(z_event, w, turn, 0),
            functools.partial(z_event, w, turn, 1),
            functools.partial(x_event, w, turn),
            functools.partial(z_event, w, turn, 2),
            functools.partial(y_event, w, turn),
            functools.partial(z_event, w, turn, 3),
        ]

    def came(w, turn, o):
        if o != 0:
            x_came(w, turn, o)
        else:
            y_came(w, turn, 3)
        if o != 1:
            y_came(w, turn, o)
        else:
            x_came(w, turn, 3)

    def complete(w, rank, o):
        for turn in ((1, 2) if rank else (0,)):
            came(w, turn, o)

    def settle(w):
        for k in range(4):
            @pl.when(has_up)
            def _():
                z_copy(w, row, k, 3, True, row - 1).wait_send()

            @pl.when(has_down)
            def _():
                z_copy(w, row, k, 4, True, row + 1).wait_send()

            for turn in range(3):
                up, down = relays(turn)

                @pl.when(jnp.logical_or(up, down))
                def _():
                    z_copy(w, turns[turn], k, turn, False, row).wait_send()

        for turn in range(3):
            for i in range(4):
                x_copy(w, turn, i).wait_send()
                y_copy(w, turn, i).wait_send()

    barrier = pltpu.get_barrier_semaphore()

    def greet(**where):
        pl.semaphore_signal(barrier, inc=1, device_id=where, device_id_type=pl.DeviceIdType.MESH)

    greet(**{CORE: other})
    greet(**{CHIPS: beside})
    greet(**{CHIPS: across})

    @pl.when(has_up)
    def _():
        greet(**{ROWS: row - 1})

    @pl.when(has_down)
    def _():
        greet(**{ROWS: row + 1})

    pl.semaphore_wait(barrier, 3 + (row + rows - 1) // rows + (2 * rows - 2 - row) // rows)

    mine_in = views.at[1, pl.ds(here, mine), 1 : band + 1]
    keep = pltpu.make_async_copy(frames, mine_in, local.at[0])
    hold_in = pltpu.make_async_copy(win.at[:, core], full_in.at[near, :, row % 2], local.at[1])
    hold_out = pltpu.make_async_copy(wout.at[:, :, :, core], full_out.at[:, :, near, :, row % 2], local.at[2])
    hold_start = pltpu.make_async_copy(start, started, local.at[3])
    swap = remote(frames, mine_in, swap_send, swap_recv, **{CORE: other})
    theirs_in = views.at[1, pl.ds(there, mine), 1 : band + 1]

    def halo(side, start):
        at = views.at[1, pl.ds(here, mine), band + 1 if side == 0 else 0]
        src = frames.at[:, 0 if side == 0 else band - 1]
        return remote(src, at, halo_send.at[side], halo_recv.at[side], **{ROWS: row - 1 if side == 0 else row + 1})

    def halo_at(side, first):
        return views.at[1, pl.ds(first, mine), band + 1 if side == 0 else 0]

    def halo_came(side):
        ref = halo_at(side, here)
        remote(ref, ref, halo_send.at[side], halo_recv.at[side], **{ROWS: row}).wait_recv()

    def handed(side, first):
        ref = halo_at(side, first)
        return remote(ref, ref, pass_send.at[side], pass_recv.at[side], **{CORE: other})

    gives = (has_up, has_down)
    takes = (has_down, has_up)

    send_own(0, range(4))
    held_back = (jnp.logical_and(inner, mate_up), jnp.logical_and(inner, jnp.logical_not(mate_up)))
    for side in range(2):
        @pl.when(jnp.logical_and(gives[side], jnp.logical_not(held_back[side])))
        def _():
            halo(side, True).start()

    swap.start()
    keep.start()

    small = [
        pltpu.make_async_copy(src, dst, local.at[4 + i])
        for i, (src, dst) in enumerate(((rate_in, rate), (angle_in, angle), (skip_in, skip)))
    ]
    for copy in small:
        copy.start()
    hold_in.start()
    hold_out.start()

    @pl.when(chip == 0)
    def _():
        hold_start.start()

    blank = jnp.zeros((columns, channels), views.dtype)
    for side in range(2):
        edge = band + 1 if side == 0 else 0

        @pl.when(jnp.logical_not(takes[side]))
        def _():
            @pl.loop(0, many)
            def _(f):
                views[1, f, edge] = blank
                for slot in range(2):
                    held[slot, 1, f, edge] = blank[:, : 2 * lanes]

    place = lax.broadcasted_iota(jnp.int32, (columns, 1), 0)
    not_first, not_last = place > 0, place < columns - 1

    def sides(wide):
        before = jnp.where(not_first, pltpu.roll(wide, 1, 0), 0.0)
        after = jnp.where(not_last, pltpu.roll(wide, columns - 1, 0), 0.0)
        return before.astype(views.dtype), after.astype(views.dtype)

    def spread_views(first):
        @pl.loop(0, mine)
        def _(i):
            f = first + i

            @pl.loop(1, band + 1)
            def _(r):
                views[0, f, r], views[2, f, r] = sides(views[1, f, r].astype(jnp.float32))

    def spread_edges(first):
        @pl.loop(0, mine)
        def _(i):
            f = first + i
            for r in (0, band + 1):
                views[0, f, r], views[2, f, r] = sides(views[1, f, r].astype(jnp.float32))

    def hand_over():
        for side in range(2):
            @pl.when(takes[side])
            def _():
                halo_came(side)
                handed(side, here).start()

        spread_edges(here)

    def take_over():
        for side in range(2):
            @pl.when(takes[side])
            def _():
                handed(side, there).wait_recv()

        spread_edges(there)

    def drive(rank, o, m0, m1):
        slot, a = slots[rank], ORDER[o]

        @pl.loop(m0, m1)
        def _(m):
            at = pl.ds(m * 2, 2)
            pixels = 2 * band * columns
            window = jnp.concatenate(
                [views[b, at, a : a + band].reshape(pixels, channels) for b in range(3)], axis=1
            )
            weight = full_in[slot, :, :, :, :, a * depth : (a + 1) * depth].reshape(2 * lanes, depth)
            result = lax.dot_general(
                window, weight, (((1,), (1,)), ((), ())), preferred_element_type=jnp.float32
            ).reshape(2, band, columns, 2 * lanes)
            if o == 0:
                driven[slot, at] = result
            else:
                driven[slot, at] += result

    blocks = many // 2

    low = lax.broadcasted_iota(jnp.int32, (1, lanes), 1) < lanes // 2

    def joined(first, second):
        first = jnp.where(core == 0, first, pltpu.roll(first, lanes // 2, 1))
        second = jnp.where(core == 0, pltpu.roll(second, lanes // 2, 1), second)
        return jnp.where(low, first, second)

    def factors(rank):
        def lane_row(ref):
            first, second = (
                jnp.broadcast_to(ref[pl.ds(2 * slots[rank] + j, 1), :], (8, lanes)) for j in range(2)
            )
            return joined(first, second)[:1]

        modulus, turn = jnp.exp(-lane_row(rate)), lane_row(angle)
        return modulus * jnp.cos(turn), modulus * jnp.sin(turn)

    def prepare():
        @pl.when(chip == 0)
        def _():
            hold_start.wait()

            @pl.loop(0, band)
            def _(r):
                for pair in range(2):
                    for part in range(2):
                        at = slice(part * lanes, (part + 1) * lanes)
                        begin[pair, r, :, at] = joined(
                            started[r, :, 4 * pair + part], started[r, :, 4 * pair + 2 + part]
                        )

        @pl.when(chip > 0)
        def _():
            @pl.loop(0, band)
            def _(r):
                for pair in range(2):
                    begin[pair, r] = jnp.zeros((columns, 2 * lanes), jnp.float32)

    def ends(rank):
        slot = slots[rank]
        lam_re, lam_im = factors(rank)

        @pl.loop(0, band)
        def _(r):
            re, im = begin[slot, r, :, :lanes], begin[slot, r, :, lanes:]
            for t in range(many):
                re, im = (
                    lam_re * re - lam_im * im + driven[slot, t, r, :, :lanes],
                    lam_re * im + lam_im * re + driven[slot, t, r, :, lanes:],
                )
            tail[slot, r, :, :lanes] = re
            tail[slot, r, :, lanes:] = im
            tail_half[slot, r, :, :lanes] = re.astype(tail_half.dtype)
            tail_half[slot, r, :, lanes:] = im.astype(tail_half.dtype)

    tells, hears = chip < 3, chip != 2
    joins = chip < 2

    def first_copy(rank):
        slot = slots[rank]
        return remote(
            tail_half.at[slot], met.at[slot], first_send.at[rank], first_recv.at[rank], **{CHIPS: beside}
        )

    def second_copy(rank):
        slot = slots[rank]
        return remote(
            joint.at[slot], far_joint.at[slot], second_send.at[rank], second_recv.at[rank], **{CHIPS: across}
        )

    def tell(rank):
        @pl.when(tells)
        def _():
            first_copy(rank).start()

    def merge(rank):
        slot = slots[rank]
        lam_re, lam_im = factors(rank)
        jump_re, jump_im = power(lam_re, lam_im, many)

        def combine(r, late_re, late_im, early_re, early_im):
            return (
                late_re + jump_re * early_re - jump_im * early_im,
                late_im + jump_re * early_im + jump_im * early_re,
            )

        def split(ref, r):
            return ref[slot, r, :, :lanes].astype(jnp.float32), ref[slot, r, :, lanes:].astype(jnp.float32)

        def put(ref, r, value):
            ref[slot, r, :, :lanes] = value[0].astype(ref.dtype)
            ref[slot, r, :, lanes:] = value[1].astype(ref.dtype)

        @pl.when(hears)
        def _():
            first_copy(rank).wait_recv()

        @pl.when(chip == 0)
        def _():
            @pl.loop(0, band)
            def _(r):
                put(joint, r, combine(r, *split(met, r), *split(tail, r)))
                put(tail, r, split(begin, r))

        @pl.when(chip == 1)
        def _():
            @pl.loop(0, band)
            def _(r):
                put(joint, r, combine(r, *split(tail, r), *split(met, r)))
                put(tail, r, split(met, r))

        @pl.when(joins)
        def _():
            second_copy(rank).start()

    def carry(rank):
        slot = slots[rank]
        lam_re, lam_im = factors(rank)
        jump_re, jump_im = power(lam_re, lam_im, many)

        @pl.when(jnp.logical_not(joins))
        def _():
            second_copy(rank).wait_recv()

        @pl.when(chip == 2)
        def _():
            @pl.loop(0, band)
            def _(r):
                tail[slot, r] = far_joint[slot, r].astype(jnp.float32)

        @pl.when(chip == 3)
        def _():
            @pl.loop(0, band)
            def _(r):
                late, early = met[slot, r].astype(jnp.float32), far_joint[slot, r].astype(jnp.float32)
                re, im = early[:, :lanes], early[:, lanes:]
                tail[slot, r, :, :lanes] = late[:, :lanes] + jump_re * re - jump_im * im
                tail[slot, r, :, lanes:] = late[:, lanes:] + jump_re * im + jump_im * re

    def scan_rows(rank, start, count, stride):
        slot = slots[rank]
        lam_re, lam_im = factors(rank)

        @pl.loop(0, count)
        def _(i):
            r = start + i * stride
            re, im = tail[slot, r, :, :lanes], tail[slot, r, :, lanes:]
            for t in range(many):
                re, im = (
                    lam_re * re - lam_im * im + driven[slot, t, r, :, :lanes],
                    lam_re * im + lam_im * re + driven[slot, t, r, :, lanes:],
                )
                for part, value in enumerate((re, im)):
                    at = slice(part * lanes, (part + 1) * lanes)
                    before, after = sides(value)
                    held[slot, 0, t, 1 + r, :, at] = before
                    held[slot, 1, t, 1 + r, :, at] = value.astype(held.dtype)
                    held[slot, 2, t, 1 + r, :, at] = after

    def edge_copy(rank, side):
        slot = slots[rank]
        return remote(
            held.at[slot, 1, :, 1 if side == 0 else band],
            held.at[slot, 1, :, band + 1 if side == 0 else 0],
            edge_send.at[rank, side],
            edge_recv.at[slot, side],
            **{ROWS: row - 1 if side == 0 else row + 1},
        )

    def scan(rank):
        scan_rows(rank, 0, 2, band - 1)
        scan_rows(rank, 1, (band - 2) // 2, 1)
        for side in range(2):
            @pl.when(gives[side])
            def _():
                edge_copy(rank, side).start()
        scan_rows(rank, 1 + (band - 2) // 2, band - 2 - (band - 2) // 2, 1)

    def edges_came(rank):
        slot = slots[rank]
        for side in range(2):
            at = band + 1 if side == 0 else 0
            ref = held.at[slot, 1, :, at]

            @pl.when(takes[side])
            def _():
                remote(
                    ref, ref, edge_send.at[rank, side], edge_recv.at[slot, side], **{ROWS: row}
                ).wait_recv()

            @pl.loop(0, many)
            def _(f):
                held[slot, 0, f, at], held[slot, 2, f, at] = sides(held[slot, 1, f, at].astype(jnp.float32))

    def mix_block(rank, rights, first, fresh):
        slot = slots[rank]
        pixels = 2 * band * columns
        window = jnp.concatenate(
            [
                held[slot, b, pl.ds(first, 2), a : a + band].reshape(pixels, 2 * lanes)
                for a in rights
                for b in range(3)
            ],
            axis=1,
        )
        weight = jnp.concatenate([full_out[a, :, slot].reshape(6 * lanes, channels) for a in rights], axis=0)
        result = jnp.dot(window, weight, preferred_element_type=jnp.float32)
        result = result.reshape(2, band, columns, channels)
        if fresh:
            return result
        return acc[pl.ds(first, 2)] + result

    def mix(rank, rights, fresh, m0=0, m1=None):
        @pl.loop(m0, blocks if m1 is None else m1)
        def _(m):
            acc[pl.ds(m * 2, 2)] = mix_block(rank, rights, m * 2, fresh)

    def part_copy(m):
        at = pl.ds(m * 2, 2)
        return remote(
            given.at[at], got.at[at], part_send.at[m], part_recv.at[m], **{CORE: other}
        )

    def out_copy(f):
        return pltpu.make_async_copy(done.at[f], out.at[f], out_sem.at[f])

    def mix_last(rank, rights):
        for m in range(blocks // 2):
            given[m * 2 : m * 2 + 2] = mix_block(rank, rights, there + m * 2, False).astype(given.dtype)
            part_copy(m).start()
        for m in range(blocks // 2):
            acc[pl.ds(here + m * 2, 2)] = mix_block(rank, rights, here + m * 2, False)
        for m in range(blocks // 2):
            part_copy(m).wait_recv()

            @pl.loop(0, 2)
            def _(i):
                f = m * 2 + i

                @pl.loop(0, band)
                def _(r):
                    value = acc[here + f, r] + got[f, r].astype(jnp.float32)
                    value = value + skip[...] * views[1, here + f, 1 + r].astype(jnp.float32)
                    done[f, r] = (0.5 * value * (1.0 + lax.erf(value * 0.7071067811865476))).astype(done.dtype)

                out_copy(f).start()

    steps = iter(events(0, 0))
    next(steps)()
    next(steps)()

    @pl.when(inner)
    def _():
        bring(0, 1, 0)
        bring(0, 1, 1)
        for side in range(2):
            @pl.when(held_back[side])
            def _():
                halo(side, True).start()

    keep.wait()
    spread_views(here)
    next(steps)()
    next(steps)()
    prepare()
    next(steps)()
    next(steps)()
    remote(theirs_in, theirs_in, swap_send, swap_recv, **{CORE: other}).wait_recv()
    spread_views(there)
    hold_in.wait()
    hold_out.wait()
    for copy in small:
        copy.wait()
    half = blocks // 2

    @pl.when(inner)
    def _():
        fan(0, 1, 0)
        bring(0, 1, 2)
        bring(0, 1, 3)
        fan(0, 1, 1)
        complete(0, 0, 0)
        drive(0, 0, 0, half)
        fan(0, 1, 2)
        drive(0, 0, half, blocks)
        hand_over()
        z_event(0, 2, 0)
        x_event(0, 1)
        take_over()
        complete(0, 0, 1)
        drive(0, 1, 0, half)
        z_event(0, 2, 1)
        y_event(0, 1)
        drive(0, 1, half, blocks)
        z_event(0, 2, 2)
        z_event(0, 2, 3)
        send_early(1)
        send_late(1, 0)
        complete(0, 0, 2)
        drive(0, 2, 0, blocks)
        ends(0)
        x_event(0, 2)
        y_event(0, 2)
        tell(0)
        complete(0, 1, 0)
        drive(1, 0, 0, blocks)
        send_late(1, 1)
        bring(1, 0, 2)
        bring(1, 0, 3)
        bring(1, 0, 0)
        bring(1, 0, 1)
        fan(1, 0, 0)
        complete(0, 1, 1)
        drive(1, 1, 0, blocks)
        merge(0)
        complete(0, 1, 2)
        drive(1, 2, 0, blocks)
        ends(1)
        tell(1)
        bring(1, 1, 0)
        bring(1, 1, 1)
        bring(1, 1, 2)
        bring(1, 1, 3)
        fan(1, 0, 1)
        carry(0)
        scan(0)
        bring(1, 2, 2)
        bring(1, 2, 3)
        merge(1)
        fan(1, 0, 2)
        x_event(1, 0)
        fan(1, 1, 0)
        y_event(1, 0)
        fan(1, 1, 1)
        bring(1, 2, 0)
        bring(1, 2, 1)
        fan(1, 1, 2)
        carry(1)
        scan(1)
        complete(1, 0, 0)
        mix(0, (1,), True)
        x_event(1, 1)
        fan(1, 2, 2)
        edges_came(0)
        complete(1, 0, 1)
        mix(0, (0,), False)
        y_event(1, 1)
        fan(1, 2, 0)
        fan(1, 2, 1)
        complete(1, 0, 2)
        mix(0, (2,), False)
        edges_came(1)
        complete(1, 1, 2)
        mix(1, (2,), False, 0, half)
        x_event(1, 2)
        mix(1, (2,), False, half)
        y_event(1, 2)
        complete(1, 1, 0)
        mix(1, (1,), False)
        complete(1, 1, 1)

    @pl.when(jnp.logical_not(inner))
    def _():
        z_event(0, 1, 0)
        complete(0, 0, 0)
        drive(0, 0, 0, half)
        z_event(0, 1, 1)
        drive(0, 0, half, blocks)
        x_event(0, 1)
        hand_over()
        take_over()
        complete(0, 0, 1)
        drive(0, 1, 0, half)
        z_event(0, 1, 2)
        send_early(1)
        drive(0, 1, half, blocks)
        y_event(0, 1)
        z_event(0, 1, 3)
        complete(0, 0, 2)
        drive(0, 2, 0, half)
        z_event(0, 2, 0)
        drive(0, 2, half, blocks)
        z_event(0, 2, 1)
        ends(0)
        x_event(0, 2)
        z_event(0, 2, 2)
        y_event(0, 2)
        tell(0)
        complete(0, 1, 0)
        drive(1, 0, 0, blocks)
        z_event(0, 2, 3)
        bring(1, 0, 0)
        fan(1, 0, 0)
        complete(0, 1, 1)
        drive(1, 1, 0, blocks)
        merge(0)
        bring(1, 0, 1)
        fan(1, 0, 1)
        complete(0, 1, 2)
        drive(1, 2, 0, blocks)
        ends(1)
        tell(1)
        carry(0)
        scan(0)
        bring(1, 0, 2)
        fan(1, 0, 2, x=False)
        merge(1)
        fan(1, 0, 2, y=False)
        x_event(1, 0)
        bring(1, 0, 3)
        z_event(1, 1, 0)
        y_event(1, 0)
        z_event(1, 1, 1)
        carry(1)
        scan(1)
        z_event(1, 1, 2)
        complete(1, 0, 0)
        mix(0, (1,), True, 0, half)
        x_event(1, 1)
        mix(0, (1,), True, half)
        z_event(1, 1, 3)
        z_event(1, 2, 2)
        edges_came(0)
        complete(1, 0, 1)
        mix(0, (0,), False, 0, half)
        z_event(1, 2, 3)
        y_event(1, 1)
        mix(0, (0,), False, half)
        z_event(1, 2, 0)
        complete(1, 0, 2)
        mix(0, (2,), False, 0, half)
        z_event(1, 2, 1)
        mix(0, (2,), False, half)
        x_event(1, 2)
        edges_came(1)
        complete(1, 1, 2)
        mix(1, (2,), False, 0, half)
        y_event(1, 2)
        mix(1, (2,), False, half)
        complete(1, 1, 0)
        mix(1, (1,), False)
        complete(1, 1, 1)

    mix_last(1, (0,))
    settle(0)
    settle(1)
    swap.wait_send()
    for side in range(2):
        @pl.when(gives[side])
        def _():
            halo(side, False).wait_send()
            for rank in range(2):
                edge_copy(rank, side).wait_send()

        @pl.when(takes[side])
        def _():
            handed(side, here).wait_send()

    for rank in range(2):
        @pl.when(tells)
        def _():
            first_copy(rank).wait_send()

        @pl.when(joins)
        def _():
            second_copy(rank).wait_send()

    for m in range(blocks // 2):
        part_copy(m).wait_send()

    for f in range(mine):
        out_copy(f).wait()


def layer(weight_in, weight_out, frames_in, start, log_decay, rotation, skip_gain):
    count, band, columns, channels = frames_in.shape
    lanes = weight_in.shape[1]
    quarter = lanes // 8
    many = 2 * count
    anywhere = pl.BlockSpec(memory_space=pl.ANY)
    dma = pltpu.SemaphoreType.DMA
    half = frames_in.dtype
    full = jnp.float32
    return pl.pallas_call(
        layer_kernel,
        out_shape=jax.ShapeDtypeStruct(frames_in.shape, half),
        in_specs=[anywhere] * 7,
        out_specs=anywhere,
        scratch_shapes=[
            pltpu.VMEM((log_decay.size // lanes, lanes), full),
            pltpu.VMEM((log_decay.size // lanes, lanes), full),
            pltpu.VMEM((1, channels), full),
            pltpu.VMEM(frames_in.shape, half),
            pltpu.VMEM(start.shape, full),
            pltpu.VMEM((2, band, columns, 2 * lanes), full),
            pltpu.VMEM((3, many, band + 2, columns, channels), half),
            pltpu.VMEM((2, 2, 2, 4, quarter, 9 * channels), half),
            pltpu.VMEM((3, 3, 2, 2, 2, 4, quarter, channels), half),
            pltpu.VMEM((2, many, band, columns, 2 * lanes), full),
            pltpu.VMEM((2, 3, many, band + 2, columns, 2 * lanes), half),
            pltpu.VMEM((many, band, columns, channels), full),
            pltpu.VMEM((2, band, columns, 2 * lanes), full),
            pltpu.VMEM((2, band, columns, 2 * lanes), half),
            pltpu.VMEM((2, band, columns, 2 * lanes), half),
            pltpu.VMEM((2, band, columns, 2 * lanes), half),
            pltpu.VMEM((2, band, columns, 2 * lanes), half),
            pltpu.VMEM((count, band, columns, channels), half),
            pltpu.VMEM((count, band, columns, channels), half),
            dma((2, 5, 4)), dma((2, 4, 4)), dma((2, 3, 4)), dma((2, 3, 4)), dma((2, 3, 4)), dma((2, 3, 4)),
            dma((2,)), dma((2,)), dma((2,)), dma((2,)), dma((2, 2)), dma((2, 2)),
            dma((2,)), dma((2,)), dma((2,)), dma((2,)), dma, dma,
            dma((many // 4,)), dma((many // 4,)), dma((7,)), dma((count,)),
        ],
        compiler_params=pltpu.CompilerParams(
            collective_id=3, has_side_effects=True, vmem_limit_bytes=63 * 1024 * 1024
        ),
    )(
        weight_in.reshape(2, 2, 4, quarter, 9 * channels),
        weight_out.reshape(3, 3, 2, 2, 4, quarter, channels),
        frames_in,
        start,
        log_decay.reshape(-1, lanes),
        rotation.reshape(-1, lanes),
        skip_gain.reshape(1, channels),
    )


def fused(frames_in, weight_in, weight_out, log_decay, rotation, start_state, skip_gain):
    lanes = weight_in.shape[1]
    band, columns = start_state.shape[:2]
    start = start_state.reshape(band, columns, 2, -1, lanes).swapaxes(2, 3).reshape(band, columns, -1, lanes)
    return layer(weight_in, weight_out, frames_in, start, log_decay, rotation, skip_gain)


def fits(frames_in, weight_in):
    count, band, columns, channels = frames_in.shape
    chips, cores, rows = (lax.axis_size(a) for a in (CHIPS, CORE, ROWS))
    return (
        (chips, rows) == (4, 2 * cores)
        and weight_in.shape[1] % 128 == 0
        and channels % 128 == 0
        and columns % 16 == 0
        and band >= 4
        and count % 4 == 0
    )


def on_device(frames_in, weight_in, weight_out, log_decay, rotation, start_state, skip_gain):
    if fits(frames_in, weight_in):
        return fused(frames_in, weight_in, weight_out, log_decay, rotation, start_state, skip_gain)
    frame_count, band_rows, columns, channels = frames_in.shape
    shard = weight_in.shape[1]
    chips, cores, rows = (lax.axis_size(a) for a in (CHIPS, CORE, ROWS))
    core, chip = lax.axis_index(CORE), lax.axis_index(CHIPS)
    half = shard // cores
    many = chips // 2
    piece = half // (2 * many)

    def own(vector, axis):
        picks = [
            jnp.concatenate(
                [
                    lax.slice_in_dim(vector, r * shard + c * half, r * shard + (c + 1) * half, axis=axis)
                    for r in range(rows)
                ],
                axis=axis,
            )
            for c in range(cores)
        ]
        return jnp.where(core == 0, picks[0], picks[1])

    states = rows * half
    slice_in = lax.dynamic_slice_in_dim(weight_in, core * half, half, 1)
    slice_out = lax.dynamic_slice_in_dim(weight_out, core * half, half, 2)
    own_in = slice_in.reshape(2, many, 2, piece, 9 * channels)
    own_out = slice_out.reshape(9, 2, many, 2, piece, channels)

    mine = with_halo(frames_in)
    theirs = swapped(mine)
    first = jnp.where(core == 0, mine, theirs)
    second = jnp.where(core == 0, theirs, mine)
    field = jnp.concatenate([first, second], axis=0)
    total = field.shape[0]

    if piece % 16 == 0 and total % GROUPS == 0:
        both, out_full = drive(own_in, own_out, field, chips, rows)
        both = both.reshape(total, band_rows, columns, 2 * states)
    else:
        in_full = spread(own_in, 0, chips, rows, 0).reshape(2, states, 3, 3, channels)
        out_full = spread(own_out, 1, chips, rows, 1)
        both = jnp.concatenate(
            [conv(field, in_full[part], "OHWI") for part in range(2)], axis=-1
        )

    log_rate, angle = own(log_decay, 0), own(rotation, 0)
    start = own(start_state, 3)
    lam_re, lam_im = powers(log_rate, angle, jnp.float32(1.0))
    begin = jnp.concatenate([start[:, :, 0], start[:, :, 1]], axis=-1)
    begin = jnp.where(chip == 0, begin, jnp.float32(0.0))
    factor = jnp.stack([lam_re, lam_im])
    tail = recur(both, begin, factor, True)
    carry_re = carry_im = jnp.float32(0.0)
    for step in range(1, chips):
        far = shifted(tail, CHIPS, step).astype(jnp.float32)
        jump_re, jump_im = powers(log_rate, angle, jnp.float32(total * (step - 1)))
        carry_re = carry_re + jump_re * far[..., :states] - jump_im * far[..., states:]
        carry_im = carry_im + jump_re * far[..., states:] + jump_im * far[..., :states]
    begin = begin + jnp.concatenate([carry_re, carry_im], axis=-1)
    held = with_halo(recur(both, begin, factor, False))

    out_weight = out_full.reshape(3, 3, 2 * states, channels)
    held_theirs = lax.dynamic_slice_in_dim(held, (1 - core) * frame_count, frame_count, 0)
    held_mine = lax.dynamic_slice_in_dim(held, core * frame_count, frame_count, 0)
    sent = conv(held_theirs, out_weight, "HWIO").astype(jnp.bfloat16)
    got = swapped(sent).astype(jnp.float32)
    mixing = conv(held_mine, out_weight, "HWIO") + got
    pre_act = mixing + skip_gain * frames_in.astype(jnp.float32)
    return jax.nn.gelu(pre_act, approximate=False).astype(jnp.bfloat16)


def solution(mesh):
    count, rows = mesh.devices.shape
    fine = Mesh(mesh.devices.reshape(count // 2, 2, rows), (CHIPS, CORE, ROWS))
    frames = P((CHIPS, CORE), ROWS, None, None)
    return jax.shard_map(
        on_device,
        mesh=fine,
        in_specs=(
            frames,
            P(None, ROWS, None),
            P(None, None, ROWS, None),
            P(),
            P(),
            P(ROWS, None, None, None),
            P(),
        ),
        out_specs=frames,
        check_vma=False,
    )
```
